256 devices in a mesh: dom: 128 (over x, y, z), col: 2 (over core).
Axes of the slice: x: 4, y: 4, z: 8, core: 2. Of those that a mesh axis runs over, the one named last changes fastest.
Arguments:
- features: bfloat16 [196608, 512], P('dom', 'col'), may hold values from -6 to 6
- cotangent: bfloat16 [196608, 512], P('dom', 'col'), may hold values from -6 to 6
- w_self: bfloat16 [512, 512], P('col'), may hold values from -0.25 to 0.25
- w_neigh: bfloat16 [512, 512], P('col'), may hold values from -0.25 to 0.25
- hub_rows: int32 [4096], P('dom'), may hold values from 0 to 1535, as said below
- send_rows: int32 [128, 128, 32], P('dom'), may hold values from 0 to 1535
- neighbours: int32 [196608, 12], P('dom'), may hold values from 0 to 9727, as said below
- counts: int32 [196608], P('dom'), may hold values from 8 to 12
Outputs:
- layer_out: bfloat16 [196608, 512], P('dom', 'col')
- grad_self: float32 [512, 512], P('col')
- grad_neigh: float32 [512, 512], P('col')
The draws below stay inside these ranges and needn't reach their ends.
Inputs may be any that keep to these rules, and one draw needn't show every extreme that they name: `hub_rows`: the 32 entries of one partition are distinct rows of that partition. `neighbours`: the first 8 slots of a node are always live; every hub row and every received row of the lookup table is named by some live slot in every partition.
All inputs are finite; a program needn't handle non-finite values.
Results may differ from the reference program's by a relative error of at most 0.0053.
Values may be sent and summed in bfloat16 or wider, within the bound.
No kernel may reach another device: no remote copies, remote signals or barrier semaphores. Data moves between devices by JAX's collectives and lax.ppermute only.
A program may use at most 64 MiB of HBM per device.

```python
import math
import jax
import jax.numpy as jnp
from jax import lax

H = 512
DEG = 12
MIN_DEG = 8
NODE_DEV = 1536
HUB_DEV = 32
BLK = 32
NODES = 196608
HUBS = 4096
N_DOM = 128


def draw_hub_rows(key, part):
    subkeys = jax.random.split(key, N_DOM)
    high_owner = jax.random.randint(jax.random.fold_in(key, 3), (), 0, N_DOM, dtype=jnp.int32)
    low_owner = (high_owner + 1) % N_DOM

    def per_device(subkey, owner):
        order = jax.random.permutation(subkey, NODE_DEV).astype(jnp.int32)
        target = jnp.where(owner == high_owner, NODE_DEV - 1, jnp.where(owner == low_owner, 0, order[0]))
        moved = (order + (target - order[0]) + NODE_DEV) % NODE_DEV
        return moved[:HUB_DEV].astype(jnp.int32)
    return jax.vmap(per_device)(subkeys, jnp.arange(N_DOM, dtype=jnp.int32)).reshape(HUBS)


def draw_neighbours(key, part):
    subkeys = jax.random.split(jax.random.fold_in(key, 7), N_DOM)
    special = HUBS + N_DOM * BLK

    def per_device(subkey):
        first_key, second_key, third_key = jax.random.split(subkey, 3)
        ranking = jax.random.permutation(first_key, NODE_DEV).astype(jnp.int32)
        position = ranking[:, None] * MIN_DEG + jnp.arange(MIN_DEG, dtype=jnp.int32)[None, :]
        local_pick = jax.random.randint(second_key, (NODE_DEV, MIN_DEG), 0, NODE_DEV, dtype=jnp.int32)
        leading = jnp.where(position < special, NODE_DEV + position, local_pick)
        trailing = jax.random.randint(third_key, (NODE_DEV, DEG - MIN_DEG), 0, NODE_DEV + special, dtype=jnp.int32)
        trailing = trailing.at[0, 0].set(0)
        return jnp.concatenate([leading, trailing], 1)
    return jax.vmap(per_device)(subkeys).reshape(NODES, DEG)


def draw_counts(key, part):
    subkeys = jax.random.split(jax.random.fold_in(key, 11), N_DOM)

    def per_device(subkey):
        first_key, second_key = jax.random.split(subkey, 2)
        base_count = jax.random.randint(first_key, (NODE_DEV,), MIN_DEG, DEG + 1, dtype=jnp.int32)
        chosen = jax.random.randint(second_key, (), 0, NODE_DEV, dtype=jnp.int32)
        return jnp.where(jnp.arange(NODE_DEV, dtype=jnp.int32) == chosen, DEG, base_count).astype(jnp.int32)
    return jax.vmap(per_device)(subkeys).reshape(NODES)


def plant(drawn, key, smallest, largest):
    place = [jax.random.randint(jax.random.fold_in(key, axis), (), 0, length) for axis, length in enumerate(drawn.shape)]
    main_axis = drawn.shape.index(max(drawn.shape))
    beside = place[:main_axis] + [(place[main_axis] + 1) % drawn.shape[main_axis]] + place[main_axis + 1:]
    return drawn.at[tuple(place)].set(smallest).at[tuple(beside)].set(largest)


def levels(rng, dims, cuts, low, largest):
    level, own = 1.0, jax.random.fold_in(rng, 6)
    for dim, shards_of in cuts:
        steps = jnp.exp(jax.random.uniform(jax.random.fold_in(own, dim), (shards_of,), jnp.float32, low / len(cuts), largest / len(cuts)))
        level = level * jnp.repeat(steps, dims[dim] // shards_of).reshape([-1 if axis == dim else 1 for axis in range(len(dims))])
    return level


def bell_draw(rng, extent, width, reach, cuts=(), held_as=jnp.bfloat16):
    loudness = levels(rng, extent, cuts, -0.22, 0.18) if cuts else 1.0
    entries = jax.random.normal(rng, extent, jnp.float32) * width * loudness
    return jnp.minimum(jnp.maximum(entries, -reach), reach).astype(held_as)


def setup_inputs(seed: int = 0) -> dict:
    seeds = jax.random.split(jax.random.key(seed), 9)
    features = bell_draw(seeds[0], (NODES, H), 1.0, 6.0, ((0, 128), (1, 2)))
    cotangent = bell_draw(seeds[1], (NODES, H), 1.0, 6.0, ((0, 128), (1, 2)))
    w_self = bell_draw(seeds[2], (H, H), H ** -0.5, 0.25, ((0, 2),))
    w_neigh = bell_draw(seeds[3], (H, H), H ** -0.5, 0.25, ((0, 2),))
    hub_rows = draw_hub_rows(jax.random.fold_in(seeds[8], 71), 0)
    send_rows = plant(jax.random.randint(seeds[5], (N_DOM, N_DOM, BLK), 0, NODE_DEV), jax.random.fold_in(seeds[5], 1), 0, NODE_DEV - 1).astype(jnp.int32)
    neighbours = draw_neighbours(jax.random.fold_in(seeds[8], 71), 0)
    counts = draw_counts(jax.random.fold_in(seeds[8], 71), 0)
    return {"features": features, "cotangent": cotangent, "w_self": w_self, "w_neigh": w_neigh, "hub_rows": hub_rows, "send_rows": send_rows, "neighbours": neighbours, "counts": counts}


def activation(value):
    return jax.nn.gelu(value, approximate=True)

def aggregate(lookup, slots, live):
    total = jnp.zeros((slots.shape[0], lookup.shape[1]), jnp.float32)
    for slot in range(slots.shape[1]):
        picked = lookup[slots[:, slot]].astype(jnp.float32)
        total = total + jnp.where((slot < live)[:, None], picked, 0.0)
    return (total / live[:, None].astype(jnp.float32)).astype(jnp.bfloat16)

def reference(features, cotangent, w_self, w_neigh, hub_rows, send_rows, neighbours, counts):
    owners = jnp.arange(HUBS, dtype=jnp.int32) // HUB_DEV
    hub_block = features[owners * NODE_DEV + hub_rows]
    senders = jnp.arange(N_DOM, dtype=jnp.int32)[:, None] * NODE_DEV
    own_rows = features.reshape(N_DOM, NODE_DEV, H)

    def per_partition(inputs):
        local_rows, requests, slots, live = inputs
        received = features[(senders + requests).reshape(-1)]
        lookup = jnp.concatenate([local_rows, hub_block, received], 0)
        return aggregate(lookup, slots, live)
    merged = lax.map(per_partition, (own_rows, jnp.transpose(send_rows, (1, 0, 2)), neighbours.reshape(N_DOM, NODE_DEV, DEG), counts.reshape(N_DOM, NODE_DEV)))
    neigh_mean = merged.reshape(NODES, H)
    pre = jnp.dot(features, w_self, preferred_element_type=jnp.float32) + jnp.dot(neigh_mean, w_neigh, preferred_element_type=jnp.float32)
    layer_out = activation(pre).astype(jnp.bfloat16)
    _, pullback = jax.vjp(activation, pre)
    grad_pre = pullback(cotangent.astype(jnp.float32))[0].astype(jnp.bfloat16)
    factor = 1.0 / math.sqrt(NODES)
    grad_self = jnp.dot(features.T, grad_pre, preferred_element_type=jnp.float32) * factor
    grad_neigh = jnp.dot(neigh_mean.T, grad_pre, preferred_element_type=jnp.float32) * factor
    return (layer_out, grad_self, grad_neigh)
```

```python
import math

import jax
import jax.numpy as jnp
from jax import lax
from jax.sharding import PartitionSpec as P

SWAP = [(0, 1), (1, 0)]


def activation(value):
    return jax.nn.gelu(value, approximate=True)


def aggregate(lookup, slots, live):
    total = jnp.zeros((slots.shape[0], lookup.shape[1]), jnp.float32)
    for slot in range(slots.shape[1]):
        picked = lookup[slots[:, slot]].astype(jnp.float32)
        total = total + jnp.where((slot < live)[:, None], picked, 0.0)
    return (total / live[:, None].astype(jnp.float32)).astype(jnp.bfloat16)


def swap(value):
    return lax.ppermute(value, "col", SWAP)


def dot(left, right):
    return jnp.dot(left, right, preferred_element_type=jnp.float32)


def shards(features, cotangent, w_self, w_neigh, hub_rows, send_rows, neighbours, counts):
    parts = lax.axis_size("dom")
    nodes, half = features.shape
    core = lax.axis_index("col")
    weights = jnp.stack([w_self, w_neigh]).reshape(2, half, 2, half)
    w_mine = lax.dynamic_index_in_dim(weights, core, 2, keepdims=False)
    w_other = swap(lax.dynamic_index_in_dim(weights, 1 - core, 2, keepdims=False))
    features_other = swap(features)

    picks = jnp.concatenate(
        [send_rows[0], jnp.broadcast_to(hub_rows[None], (parts, hub_rows.shape[0]))], 1
    ).reshape(-1)
    onehot = (picks[:, None] == jnp.arange(nodes, dtype=jnp.int32)[None, :]).astype(jnp.bfloat16)
    outgoing = dot(onehot, features).astype(jnp.bfloat16).reshape(parts, -1, half)
    incoming = lax.all_to_all(outgoing, "dom", split_axis=0, concat_axis=0, tiled=True)
    blk = send_rows.shape[2]
    own_dot = dot(features, w_mine[0]) + dot(features_other, w_other[0])

    hubs = hub_rows.shape[0]
    width = blk + hubs
    slot = neighbours - nodes
    is_hub = slot < parts * hubs
    local = jnp.where(is_hub, slot, slot - parts * hubs)
    owner = jnp.where(is_hub, local // hubs, local // blk)
    within = jnp.where(is_hub, local % hubs + blk, local % blk)
    place = jnp.where(slot < 0, neighbours, nodes + owner * width + within)
    lookup = jnp.concatenate([features, incoming.reshape(-1, half)], 0)
    neigh_mean = aggregate(lookup, place, counts)
    mean_other = swap(neigh_mean)

    pre = own_dot + dot(neigh_mean, w_mine[1]) + dot(mean_other, w_other[1])
    layer_out = activation(pre).astype(jnp.bfloat16)
    _, pullback = jax.vjp(activation, pre)
    grad_pre = pullback(cotangent.astype(jnp.float32))[0].astype(jnp.bfloat16)

    def weight_grad(rows):
        return lax.dot_general(
            rows, grad_pre, (((0,), (0,)), ((), ())), preferred_element_type=jnp.float32
        ).astype(jnp.bfloat16)

    mine = jnp.stack([weight_grad(features), weight_grad(neigh_mean)])
    other = swap(jnp.stack([weight_grad(features_other), weight_grad(mean_other)]))
    left = jnp.where(core == 0, mine, other)
    right = jnp.where(core == 0, other, mine)
    partial = jnp.concatenate([left, right], 2).reshape(parts, -1, 2 * half)
    pieces = lax.all_to_all(partial, "dom", split_axis=0, concat_axis=0, tiled=True)
    factor = 1.0 / math.sqrt(nodes * parts)
    piece = (pieces.astype(jnp.float32).sum(0) * factor).astype(jnp.bfloat16)
    sums = lax.all_to_all(
        jnp.broadcast_to(piece[None], (parts,) + piece.shape),
        "dom", split_axis=0, concat_axis=0, tiled=True,
    )
    sums = sums.reshape(2, half, 2 * half).astype(jnp.float32)
    return (layer_out, sums[0], sums[1])


def solution(mesh):
    placed = (
        P("dom", "col"),
        P("dom", "col"),
        P("col", None),
        P("col", None),
        P("dom"),
        P("dom", None, None),
        P("dom", None),
        P("dom"),
    )
    return jax.shard_map(
        shards,
        mesh=mesh,
        in_specs=placed,
        out_specs=(P("dom", "col"), P("col", None), P("col", None)),
        check_vma=False,
    )
```

```python
import functools
import math

import jax
import jax.numpy as jnp
from jax import lax
from jax.experimental import pallas as pl
from jax.experimental.pallas import tpu as pltpu
from jax.sharding import PartitionSpec as P

SWAP = [(0, 1), (1, 0)]


def activation(value):
    return jax.nn.gelu(value, approximate=True)


def incidence_kernel(widths, slots_ref, counts_ref, *rest):
    outs, (col_ref, mult_ref) = rest[:len(widths)], rest[len(widths):]
    deg, rows = slots_ref.shape
    live = lax.broadcasted_iota(jnp.int32, (deg, rows), 0) < counts_ref[...]
    slots = jnp.where(live, slots_ref[...], -1)
    mult = jnp.zeros((deg, rows), jnp.float32)
    for k in range(deg):
        mult = mult + jnp.where(slots == slots[k:k + 1, :], 1.0, 0.0)
    col_ref[...] = slots.astype(jnp.float32).T
    mult_ref[...] = mult.T

    def tile(r, _):
        r16 = pl.multiple_of(r * 16, 16)
        cols = col_ref[pl.ds(r16, 16), :]
        mults = mult_ref[pl.ds(r16, 16), :]
        want = [jnp.broadcast_to(cols[:, k:k + 1], (16, 128)).astype(jnp.int32).astype(jnp.int16) for k in range(deg)]
        vals = [jnp.broadcast_to(mults[:, k:k + 1], (16, 128)).astype(jnp.bfloat16) for k in range(deg)]
        lane = lax.broadcasted_iota(jnp.int32, (16, 128), 1).astype(jnp.int16)
        base = 0
        for out, width in zip(outs, widths):
            for t in range(width // 128):
                here = lane + jnp.int16(base + t * 128)
                acc = jnp.zeros((16, 128), jnp.bfloat16)
                for k in range(deg):
                    acc = jnp.where(want[k] == here, vals[k], acc)
                out[pl.ds(r16, 16), t * 128:(t + 1) * 128] = acc
            base += width
        return 0
    lax.fori_loop(0, rows // 16, tile, 0)

def incidence(slots_t, counts, widths, block=128):
    deg, nodes = slots_t.shape
    total = sum(widths)
    return pl.pallas_call(
        functools.partial(incidence_kernel, widths),
        grid=(nodes // block,),
        in_specs=[pl.BlockSpec((deg, block), lambda i: (0, i)), pl.BlockSpec((1, block), lambda i: (0, i))],
        out_specs=[pl.BlockSpec((block, w), lambda i: (i, 0)) for w in widths],
        out_shape=[jax.ShapeDtypeStruct((nodes, w), jnp.bfloat16) for w in widths],
        scratch_shapes=[pltpu.VMEM((block, deg), jnp.float32)] * 2,
        cost_estimate=pl.CostEstimate(flops=2 * nodes * total * deg, bytes_accessed=2 * nodes * total, transcendentals=0),
        compiler_params=pltpu.CompilerParams(vmem_limit_bytes=40 << 20),
        name="incidence",
    )(slots_t, counts.reshape(1, nodes))


def mean_kernel(table_ref, weight_ref, start_ref, counts_ref, out_ref):
    rows = out_ref.shape[0]
    live = jnp.broadcast_to(counts_ref[...].astype(jnp.float32), (8, rows)).T[:, :1]
    total = start_ref[...] + jnp.dot(
        weight_ref[...], table_ref[...], preferred_element_type=jnp.float32
    )
    out_ref[...] = (total / live).astype(jnp.bfloat16)


def finish_mean(table, weight, start, counts, block=256):
    nodes, depth = weight.shape
    width = table.shape[1]
    return pl.pallas_call(
        mean_kernel,
        grid=(nodes // block,),
        in_specs=[
            pl.BlockSpec((depth, width), lambda i: (0, 0), pipeline_mode=pl.Buffered(1)),
            pl.BlockSpec((block, depth), lambda i: (i, 0)),
            pl.BlockSpec((block, width), lambda i: (i, 0)),
            pl.BlockSpec((1, block), lambda i: (0, i)),
        ],
        out_specs=pl.BlockSpec((block, width), lambda i: (i, 0)),
        out_shape=jax.ShapeDtypeStruct((nodes, width), jnp.bfloat16),
        cost_estimate=pl.CostEstimate(
            flops=2 * nodes * depth * width,
            bytes_accessed=2 * (nodes * depth + depth * width + 3 * nodes * width),
            transcendentals=0,
        ),
        compiler_params=pltpu.CompilerParams(vmem_limit_bytes=32 << 20),
        name="finish_mean",
    )(table, weight, start, counts.reshape(1, nodes))


def swap(value):
    return lax.ppermute(value, "col", SWAP)


def dot(left, right):
    return jnp.dot(left, right, preferred_element_type=jnp.float32)


def shards(features, cotangent, w_self, w_neigh, hub_rows, send_rows, neighbours, counts):
    parts = lax.axis_size("dom")
    nodes, half = features.shape
    core = lax.axis_index("col")
    weights = jnp.stack([w_self, w_neigh]).reshape(2, half, 2, half)
    w_mine = lax.dynamic_index_in_dim(weights, core, 2, keepdims=False)
    w_other = swap(lax.dynamic_index_in_dim(weights, 1 - core, 2, keepdims=False))
    features_other = swap(features)

    picks = jnp.concatenate(
        [send_rows[0], jnp.broadcast_to(hub_rows[None], (parts, hub_rows.shape[0]))], 1
    ).reshape(-1)
    onehot = (picks[:, None] == jnp.arange(nodes, dtype=jnp.int32)[None, :]).astype(jnp.bfloat16)
    outgoing = dot(onehot, features).astype(jnp.bfloat16).reshape(parts, -1, half)
    incoming = lax.all_to_all(outgoing, "dom", split_axis=0, concat_axis=0, tiled=True)
    blk = send_rows.shape[2]
    own_dot = dot(features, w_mine[0]) + dot(features_other, w_other[0])

    hubs = hub_rows.shape[0]
    width = blk + hubs
    named = neighbours.T
    slot = named - nodes
    is_hub = slot < parts * hubs
    far = jnp.where(is_hub, slot, slot - parts * hubs)
    owner = jnp.where(is_hub, far // hubs, far // blk)
    within = jnp.where(is_hub, far % hubs + blk, far % blk)
    place = jnp.where(slot < 0, named, nodes + owner * width + within)
    near_weight, far_weight = incidence(place, counts, (nodes, parts * width))
    near_sum = dot(near_weight, features)
    neigh_mean = finish_mean(incoming.reshape(-1, half), far_weight, near_sum, counts)
    mean_other = swap(neigh_mean)

    pre = own_dot + dot(neigh_mean, w_mine[1]) + dot(mean_other, w_other[1])
    layer_out = activation(pre).astype(jnp.bfloat16)
    _, pullback = jax.vjp(activation, pre)
    grad_pre = pullback(cotangent.astype(jnp.float32))[0].astype(jnp.bfloat16)

    def weight_grad(rows):
        return lax.dot_general(
            rows, grad_pre, (((0,), (0,)), ((), ())), preferred_element_type=jnp.float32
        ).astype(jnp.bfloat16)

    mine = jnp.stack([weight_grad(features), weight_grad(neigh_mean)])
    other = swap(jnp.stack([weight_grad(features_other), weight_grad(mean_other)]))
    left = jnp.where(core == 0, mine, other)
    right = jnp.where(core == 0, other, mine)
    partial = jnp.concatenate([left, right], 2).reshape(parts, -1, 2 * half)
    pieces = lax.all_to_all(partial, "dom", split_axis=0, concat_axis=0, tiled=True)
    factor = 1.0 / math.sqrt(nodes * parts)
    piece = (pieces.astype(jnp.float32).sum(0) * factor).astype(jnp.bfloat16)
    sums = lax.all_to_all(
        jnp.broadcast_to(piece[None], (parts,) + piece.shape),
        "dom", split_axis=0, concat_axis=0, tiled=True,
    )
    sums = sums.reshape(2, half, 2 * half).astype(jnp.float32)
    return (layer_out, sums[0], sums[1])


def solution(mesh):
    placed = (
        P("dom", "col"),
        P("dom", "col"),
        P("col", None),
        P("col", None),
        P("dom"),
        P("dom", None, None),
        P("dom", None),
        P("dom"),
    )
    return jax.shard_map(
        shards,
        mesh=mesh,
        in_specs=placed,
        out_specs=(P("dom", "col"), P("col", None), P("col", None)),
        check_vma=False,
    )
```

```python
import functools
import math

import jax
import jax.numpy as jnp
from jax import lax
from jax.experimental import pallas as pl
from jax.experimental.pallas import tpu as pltpu
from jax.sharding import PartitionSpec as P

SWAP = [(0, 1), (1, 0)]
LINES = {"x": (32, 4), "y": (8, 4), "z": (1, 8)}
GROUP = 16
SPAN = 256


def activation(value):
    return jax.nn.gelu(value, approximate=True)


def incidence_kernel(slots_ref, *outs):
    slots = slots_ref[...]
    low = (slots & (SPAN - 1)).astype(jnp.float32).T
    high = slots >> 8
    lane = lax.broadcasted_iota(jnp.int32, (SPAN, SPAN), 1).astype(jnp.float32)
    owner = lax.broadcasted_iota(jnp.int32, (GROUP, SPAN), 1) & (GROUP - 1)
    own = owner == lax.broadcasted_iota(jnp.int32, (GROUP, SPAN), 0)
    one = jnp.ones((GROUP, SPAN), jnp.bfloat16)
    zero = jnp.zeros((GROUP, SPAN), jnp.bfloat16)
    for g in range(slots.shape[0]):
        right = jnp.where(low[:, g:g + 1] == lane, 1.0, 0.0).astype(jnp.bfloat16)
        mine = jnp.where(own, jnp.broadcast_to(high[g:g + 1, :], (GROUP, SPAN)), -1).astype(jnp.int16)
        first = 0
        for out in outs:
            tiles = out.shape[1] // SPAN
            left = jnp.concatenate([jnp.where(mine == jnp.int16(first + t), one, zero) for t in range(tiles)], 0)
            made = jnp.dot(left, right, preferred_element_type=jnp.float32).astype(jnp.bfloat16)
            for t in range(tiles):
                out[g * GROUP:(g + 1) * GROUP, t * SPAN:(t + 1) * SPAN] = made[t * GROUP:(t + 1) * GROUP]
            first += tiles

def incidence(slots_t, counts, widths, batch=8):
    deg, nodes = slots_t.shape
    groups = nodes // GROUP
    depth = SPAN // GROUP
    step = lax.broadcasted_iota(jnp.int32, (depth, nodes), 0)
    slots = jnp.pad(slots_t, ((0, depth - deg), (0, 0)), constant_values=-1)
    slots = jnp.where(step < counts[None, :], slots, -1)
    slots = slots.reshape(depth, groups, GROUP).transpose(1, 0, 2).reshape(groups, SPAN)
    total = sum(widths)
    block = batch * GROUP
    return pl.pallas_call(
        incidence_kernel,
        grid=(groups // batch,),
        in_specs=[pl.BlockSpec((batch, SPAN), lambda i: (i, 0))],
        out_specs=[pl.BlockSpec((block, w), lambda i: (i, 0)) for w in widths],
        out_shape=[jax.ShapeDtypeStruct((nodes, w), jnp.bfloat16) for w in widths],
        cost_estimate=pl.CostEstimate(flops=2 * nodes * total * SPAN, bytes_accessed=2 * nodes * total, transcendentals=0),
        compiler_params=pltpu.CompilerParams(vmem_limit_bytes=24 << 20),
        name="incidence",
    )(slots)


def mean_kernel(table_ref, weight_ref, start_ref, counts_ref, out_ref):
    rows = out_ref.shape[0]
    live = jnp.broadcast_to(counts_ref[...].astype(jnp.float32), (8, rows)).T[:, :1]
    total = start_ref[...] + jnp.dot(
        weight_ref[...], table_ref[...], preferred_element_type=jnp.float32
    )
    out_ref[...] = (total / live).astype(jnp.bfloat16)


def finish_mean(table, weight, start, counts, block=256):
    nodes, depth = weight.shape
    width = table.shape[1]
    return pl.pallas_call(
        mean_kernel,
        grid=(nodes // block,),
        in_specs=[
            pl.BlockSpec((depth, width), lambda i: (0, 0), pipeline_mode=pl.Buffered(1)),
            pl.BlockSpec((block, depth), lambda i: (i, 0)),
            pl.BlockSpec((block, width), lambda i: (i, 0)),
            pl.BlockSpec((1, block), lambda i: (0, i)),
        ],
        out_specs=pl.BlockSpec((block, width), lambda i: (i, 0)),
        out_shape=jax.ShapeDtypeStruct((nodes, width), jnp.bfloat16),
        cost_estimate=pl.CostEstimate(
            flops=2 * nodes * depth * width,
            bytes_accessed=2 * (nodes * depth + depth * width + 3 * nodes * width),
            transcendentals=0,
        ),
        compiler_params=pltpu.CompilerParams(vmem_limit_bytes=32 << 20),
        name="finish_mean",
    )(table, weight, start, counts.reshape(1, nodes))


def swap(value):
    return lax.ppermute(value, "col", SWAP)


def shift(value, axis, offset):
    stride, size = LINES[axis]
    pairs = []
    for source in range(128):
        here = source // stride % size
        pairs.append((source, source + ((here + offset) % size - here) * stride))
    return lax.ppermute(value, "dom", pairs)


def gather_hubs(block, slots, nodes):
    stride, size = LINES["z"]
    lines = [list(range(first, first + size)) for first in range(0, 128, size)]
    copies = jnp.broadcast_to(block[None], (size,) + block.shape)
    line = lax.all_to_all(
        copies, "dom", split_axis=0, concat_axis=0, tiled=True, axis_index_groups=lines
    ).reshape(-1, block.shape[1])
    plane = jnp.concatenate([line] + [shift(line, "y", -ahead) for ahead in (1, 2, 3)], 0)
    middle = plane.shape[0] // 2
    after, before = shift(plane, "x", -1), shift(plane, "x", 1)
    table = jnp.concatenate(
        [plane, after, shift(after[:middle], "x", -1), shift(before[middle:], "x", 1), before], 0
    )
    here = lax.axis_index("dom")
    hub = slots - nodes
    owner = hub >> 5
    ahead_x = ((owner >> 5) - (here >> 5)) & 3
    ahead_y = ((owner >> 3) - (here >> 3)) & 3
    moved = nodes + (ahead_x * 4 + ahead_y) * line.shape[0] + (hub & (line.shape[0] - 1))
    is_hub = (hub >= 0) & (hub < table.shape[0])
    return table, jnp.where(is_hub, moved, slots)


def dot(left, right):
    return jnp.dot(left, right, preferred_element_type=jnp.float32)


def shards(features, cotangent, w_self, w_neigh, hub_rows, send_rows, neighbours, counts):
    parts = lax.axis_size("dom")
    nodes, half = features.shape
    core = lax.axis_index("col")
    weights = jnp.stack([w_self, w_neigh]).reshape(2, half, 2, half)
    w_mine = lax.dynamic_index_in_dim(weights, core, 2, keepdims=False)
    w_other = swap(lax.dynamic_index_in_dim(weights, 1 - core, 2, keepdims=False))
    features_other = swap(features)

    lanes = jnp.arange(nodes, dtype=jnp.int32)[None, :]

    def pick(rows):
        onehot = (rows[:, None] == lanes).astype(jnp.bfloat16)
        return dot(onehot, features).astype(jnp.bfloat16)

    hub_block, named = gather_hubs(pick(hub_rows), neighbours.T, nodes)
    outgoing = pick(send_rows.reshape(-1)).reshape(parts, -1, half)
    incoming = lax.all_to_all(outgoing, "dom", split_axis=0, concat_axis=0, tiled=True)
    own_dot = dot(features, w_mine[0]) + dot(features_other, w_other[0])

    own_weight, hub_weight, far_weight = incidence(
        named, counts, (nodes, hub_block.shape[0], incoming.shape[0] * incoming.shape[1])
    )
    near_sum = dot(own_weight, features) + dot(hub_weight, hub_block)
    neigh_mean = finish_mean(incoming.reshape(-1, half), far_weight, near_sum, counts)
    mean_other = swap(neigh_mean)

    pre = own_dot + dot(neigh_mean, w_mine[1]) + dot(mean_other, w_other[1])
    layer_out = activation(pre).astype(jnp.bfloat16)
    _, pullback = jax.vjp(activation, pre)
    grad_pre = pullback(cotangent.astype(jnp.float32))[0].astype(jnp.bfloat16)

    def weight_grad(rows):
        return lax.dot_general(
            rows, grad_pre, (((0,), (0,)), ((), ())), preferred_element_type=jnp.float32
        ).astype(jnp.bfloat16)

    mine = jnp.stack([weight_grad(features), weight_grad(neigh_mean)])
    other = swap(jnp.stack([weight_grad(features_other), weight_grad(mean_other)]))
    left = jnp.where(core == 0, mine, other)
    right = jnp.where(core == 0, other, mine)
    partial = jnp.concatenate([left, right], 2).reshape(parts, -1, 2 * half)
    pieces = lax.all_to_all(partial, "dom", split_axis=0, concat_axis=0, tiled=True)
    factor = 1.0 / math.sqrt(nodes * parts)
    piece = (pieces.astype(jnp.float32).sum(0) * factor).astype(jnp.bfloat16)
    sums = lax.all_to_all(
        jnp.broadcast_to(piece[None], (parts,) + piece.shape),
        "dom", split_axis=0, concat_axis=0, tiled=True,
    )
    sums = sums.reshape(2, half, 2 * half).astype(jnp.float32)
    return (layer_out, sums[0], sums[1])


def solution(mesh):
    placed = (
        P("dom", "col"),
        P("dom", "col"),
        P("col", None),
        P("col", None),
        P("dom"),
        P("dom", None, None),
        P("dom", None),
        P("dom"),
    )
    return jax.shard_map(
        shards,
        mesh=mesh,
        in_specs=placed,
        out_specs=(P("dom", "col"), P("col", None), P("col", None)),
        check_vma=False,
    )
```

```python
import functools
import math

import jax
import jax.numpy as jnp
from jax import lax
from jax.experimental import pallas as pl
from jax.experimental.pallas import tpu as pltpu
from jax.sharding import PartitionSpec as P

SWAP = [(0, 1), (1, 0)]
LINES = {"x": (32, 4), "y": (8, 4), "z": (1, 8)}
GROUP = 16
SPAN = 256


def incidence_kernel(waits, offset, slots_ref, *refs):
    slots = slots_ref[...]
    low = (slots & (SPAN - 1)).astype(jnp.float32).T
    high = slots >> 8
    lane = lax.broadcasted_iota(jnp.int32, (SPAN, SPAN), 1).astype(jnp.float32)
    owner = lax.broadcasted_iota(jnp.int32, (GROUP, SPAN), 1) & (GROUP - 1)
    own = owner == lax.broadcasted_iota(jnp.int32, (GROUP, SPAN), 0)
    one = jnp.ones((GROUP, SPAN), jnp.bfloat16)
    zero = jnp.zeros((GROUP, SPAN), jnp.bfloat16)
    for g in range(slots.shape[0]):
        right = jnp.where(low[:, g:g + 1] == lane, 1.0, 0.0).astype(jnp.bfloat16)
        mine = jnp.where(own, jnp.broadcast_to(high[g:g + 1, :], (GROUP, SPAN)), -1).astype(jnp.int16)
        first = offset // SPAN
        for out in refs[waits:]:
            tiles = out.shape[1] // SPAN
            left = jnp.concatenate([jnp.where(mine == jnp.int16(first + t), one, zero) for t in range(tiles)], 0)
            made = jnp.dot(left, right, preferred_element_type=jnp.float32).astype(jnp.bfloat16)
            for t in range(tiles):
                out[g * GROUP:(g + 1) * GROUP, t * SPAN:(t + 1) * SPAN] = made[t * GROUP:(t + 1) * GROUP]
            first += tiles

def pack_slots(slots_t, counts):
    deg, nodes = slots_t.shape
    groups = nodes // GROUP
    depth = SPAN // GROUP
    step = lax.broadcasted_iota(jnp.int32, (depth, nodes), 0)
    slots = jnp.pad(slots_t, ((0, depth - deg), (0, 0)), constant_values=-1)
    slots = jnp.where(step < counts[None, :], slots, -1)
    return slots.reshape(depth, groups, GROUP).transpose(1, 0, 2).reshape(groups, SPAN)


def incidence(slots, offset, widths, after, batch=8):
    groups = slots.shape[0]
    nodes = groups * GROUP
    total = sum(widths)
    block = batch * GROUP
    return pl.pallas_call(
        functools.partial(incidence_kernel, len(after), offset),
        grid=(groups // batch,),
        in_specs=[pl.BlockSpec((batch, SPAN), lambda i: (i, 0))]
        + [pl.BlockSpec(memory_space=pl.ANY)] * len(after),
        out_specs=[pl.BlockSpec((block, w), lambda i: (i, 0)) for w in widths],
        out_shape=[jax.ShapeDtypeStruct((nodes, w), jnp.bfloat16) for w in widths],
        cost_estimate=pl.CostEstimate(flops=2 * nodes * total * 64, bytes_accessed=nodes, transcendentals=0),
        compiler_params=pltpu.CompilerParams(vmem_limit_bytes=56 << 20),
        name="incidence",
    )(slots, *after)


def mean_kernel(table_ref, weight_ref, start_ref, counts_ref, out_ref):
    rows = out_ref.shape[0]
    live = jnp.broadcast_to(counts_ref[...].astype(jnp.float32), (8, rows)).T[:, :1]
    total = start_ref[...] + jnp.dot(
        weight_ref[...], table_ref[...], preferred_element_type=jnp.float32
    )
    out_ref[...] = (total / live).astype(jnp.bfloat16)


def finish_mean(table, weight, start, counts, block=256):
    nodes, depth = weight.shape
    width = table.shape[1]
    return pl.pallas_call(
        mean_kernel,
        grid=(nodes // block,),
        in_specs=[
            pl.BlockSpec((depth, width), lambda i: (0, 0), pipeline_mode=pl.Buffered(1)),
            pl.BlockSpec((block, depth), lambda i: (i, 0)),
            pl.BlockSpec((block, width), lambda i: (i, 0)),
            pl.BlockSpec((1, block), lambda i: (0, i)),
        ],
        out_specs=pl.BlockSpec((block, width), lambda i: (i, 0)),
        out_shape=jax.ShapeDtypeStruct((nodes, width), jnp.bfloat16),
        cost_estimate=pl.CostEstimate(
            flops=2 * nodes * depth * width,
            bytes_accessed=2 * (nodes * depth + depth * width + 3 * nodes * width),
            transcendentals=0,
        ),
        compiler_params=pltpu.CompilerParams(vmem_limit_bytes=56 << 20),
        name="finish_mean",
    )(table, weight, start, counts.reshape(1, nodes))


def layer_kernel(core_ref, own, own_far, mean, mean_far, w_self, w_self_far, w_neigh, w_neigh_far,
                 cotangent_ref, out_ref, mine_ref, other_ref, total_ref):
    step = pl.program_id(0)

    def product(rows, weight):
        return jnp.dot(rows[...], weight[...], preferred_element_type=jnp.float32)

    pre = (product(own, w_self) + product(own_far, w_self_far)) + (
        product(mean, w_neigh) + product(mean_far, w_neigh_far)
    )
    scale = math.sqrt(2 / math.pi)
    square = pre * pre
    tanh = jnp.tanh(scale * (pre + 0.044715 * (square * pre)))
    half_up = 0.5 * (1.0 + tanh)
    out_ref[...] = (pre * half_up).astype(jnp.bfloat16)
    slope = half_up + 0.5 * pre * (1.0 - tanh * tanh) * (scale * (1.0 + 3 * 0.044715 * square))
    grad = (cotangent_ref[...].astype(jnp.float32) * slope).astype(jnp.bfloat16)
    part = jnp.concatenate(
        [
            lax.dot_general(
                grad, rows[...], (((0,), (0,)), ((), ())), preferred_element_type=jnp.float32
            )
            for rows in (own, mean, own_far, mean_far)
        ],
        1,
    )

    @pl.when(step == 0)
    def _():
        total_ref[...] = part

    @pl.when(step > 0)
    def _():
        total_ref[...] += part

    @pl.when(step == pl.num_programs(0) - 1)
    def _():
        total = total_ref[...].T.astype(jnp.bfloat16)
        mine_ref[...] = total[:mine_ref.shape[0]]
        other_ref[...] = total[mine_ref.shape[0]:]


def layer(core, own, own_far, mean, mean_far, w_self, w_self_far, w_neigh, w_neigh_far, cotangent, block=256):
    nodes, half = own.shape
    rows = pl.BlockSpec((block, half), lambda i, c: (i, 0))
    weight = pl.BlockSpec((half, half), lambda i, c: (0, c[0]), pipeline_mode=pl.Buffered(1))
    whole = pl.BlockSpec((2 * half, half), lambda i, c: (0, 0))
    return pl.pallas_call(
        layer_kernel,
        grid_spec=pltpu.PrefetchScalarGridSpec(
            num_scalar_prefetch=1,
            grid=(nodes // block,),
            in_specs=[rows] * 4 + [weight] * 4 + [rows],
            out_specs=[rows, whole, whole],
            scratch_shapes=[pltpu.VMEM((half, 4 * half), jnp.float32)],
        ),
        out_shape=[
            jax.ShapeDtypeStruct((nodes, half), jnp.bfloat16),
            jax.ShapeDtypeStruct((2 * half, half), jnp.bfloat16),
            jax.ShapeDtypeStruct((2 * half, half), jnp.bfloat16),
        ],
        cost_estimate=pl.CostEstimate(
            flops=16 * nodes * half * half, bytes_accessed=12 * nodes * half, transcendentals=nodes * half
        ),
        compiler_params=pltpu.CompilerParams(vmem_limit_bytes=24 << 20),
        name="layer",
    )(core, own, own_far, mean, mean_far, w_self, w_self_far, w_neigh, w_neigh_far, cotangent)


def swap(value):
    return lax.ppermute(value, "col", SWAP)


def shift(value, axis, offset):
    stride, size = LINES[axis]
    pairs = []
    for source in range(128):
        here = source // stride % size
        pairs.append((source, source + ((here + offset) % size - here) * stride))
    return lax.ppermute(value, "dom", pairs)


def gather_hubs(block, slots, nodes):
    size = LINES["z"][1]
    line = jnp.concatenate([block] + [shift(block, "z", -ahead) for ahead in range(1, size)], 0)
    plane = jnp.concatenate([line] + [shift(line, "y", -ahead) for ahead in (1, 2, 3)], 0)
    middle = plane.shape[0] // 2
    after, before = shift(plane, "x", -1), shift(plane, "x", 1)
    table = jnp.concatenate(
        [plane, after, shift(after[:middle], "x", -1), shift(before[middle:], "x", 1), before], 0
    )
    here = lax.axis_index("dom")
    hub = slots - nodes
    owner = hub >> 5
    ahead_x = ((owner >> 5) - (here >> 5)) & 3
    ahead_y = ((owner >> 3) - (here >> 3)) & 3
    ahead_z = (owner - here) & 7
    moved = nodes + (((ahead_x * 4 + ahead_y) * 8 + ahead_z) << 5) + (hub & 31)
    is_hub = (hub >= 0) & (hub < table.shape[0])
    return table, plane, jnp.where(is_hub, moved, slots)


def dot(left, right):
    return jnp.dot(left, right, preferred_element_type=jnp.float32)


def shards(features, cotangent, w_self, w_neigh, hub_rows, send_rows, neighbours, counts):
    parts = lax.axis_size("dom")
    nodes, half = features.shape
    core = lax.axis_index("col")
    features_far, w_self_far, w_neigh_far = swap(features), swap(w_self), swap(w_neigh)
    lanes = jnp.arange(nodes, dtype=jnp.int32)[None, :]

    def pick(rows):
        onehot = (rows[:, None] == lanes).astype(jnp.bfloat16)
        return dot(onehot, features).astype(jnp.bfloat16)

    outgoing = pick(send_rows.reshape(-1))
    started = jnp.minimum(jnp.abs(outgoing[0, 0]), 0).astype(jnp.int32)
    outgoing = outgoing.reshape(parts, -1, half)
    hub_block, plane, named = gather_hubs(pick(hub_rows + started), neighbours.T, nodes)
    incoming = lax.all_to_all(outgoing, "dom", split_axis=0, concat_axis=0, tiled=True)

    slots = pack_slots(named, counts)
    near = nodes + hub_block.shape[0]
    far = incoming.shape[0] * incoming.shape[1]
    (far_weight,) = incidence(slots, near, (far,), (plane, features_far, w_self_far, w_neigh_far))
    own_weight, hub_weight = incidence(slots, 0, (nodes, hub_block.shape[0]), (plane,))
    near_sum = dot(own_weight, features) + dot(hub_weight, hub_block)
    neigh_mean = finish_mean(incoming.reshape(-1, half), far_weight, near_sum, counts)
    mean_far = swap(neigh_mean)
    layer_out, mine, other = layer(
        core.astype(jnp.int32).reshape(1), features, features_far, neigh_mean, mean_far,
        w_self, w_self_far, w_neigh, w_neigh_far, cotangent,
    )
    partial = jnp.concatenate([mine, swap(other)], 0).reshape(parts, -1, half)
    pieces = lax.all_to_all(partial, "dom", split_axis=0, concat_axis=0, tiled=True)
    factor = 1.0 / math.sqrt(nodes * parts)
    piece = (pieces.astype(jnp.float32).sum(0) * factor).astype(jnp.bfloat16)
    sums = lax.all_to_all(
        jnp.broadcast_to(piece[None], (parts,) + piece.shape),
        "dom", split_axis=0, concat_axis=0, tiled=True,
    )
    sums = sums.reshape(2, 2, half, half).astype(jnp.float32)
    low = jnp.where(core == 0, sums[0], sums[1])
    high = jnp.where(core == 0, sums[1], sums[0])
    return (
        layer_out,
        jnp.concatenate([low[0], high[0]], 1),
        jnp.concatenate([low[1], high[1]], 1),
    )


def solution(mesh):
    placed = (
        P("dom", "col"),
        P("dom", "col"),
        P("col", None),
        P("col", None),
        P("dom"),
        P("dom", None, None),
        P("dom", None),
        P("dom"),
    )
    return jax.shard_map(
        shards,
        mesh=mesh,
        in_specs=placed,
        out_specs=(P("dom", "col"), P("col", None), P("col", None)),
        check_vma=False,
    )
```

```python
import functools
import math

import jax
import jax.numpy as jnp
from jax import lax
from jax.experimental import pallas as pl
from jax.experimental.pallas import tpu as pltpu
from jax.sharding import PartitionSpec as P

SWAP = [(0, 1), (1, 0)]
LINES = {"x": (32, 4), "y": (8, 4), "z": (1, 8)}
GROUP = 16
SPAN = 256


def incidence_kernel(waits, slots_ref, *refs):
    slots = slots_ref[...]
    low = (slots & (SPAN - 1)).astype(jnp.float32).T
    high = slots >> 8
    lane = lax.broadcasted_iota(jnp.int32, (SPAN, SPAN), 1).astype(jnp.float32)
    owner = lax.broadcasted_iota(jnp.int32, (GROUP, SPAN), 1) & (GROUP - 1)
    own = owner == lax.broadcasted_iota(jnp.int32, (GROUP, SPAN), 0)
    one = jnp.ones((GROUP, SPAN), jnp.bfloat16)
    zero = jnp.zeros((GROUP, SPAN), jnp.bfloat16)
    for g in range(slots.shape[0]):
        right = jnp.where(low[:, g:g + 1] == lane, 1.0, 0.0).astype(jnp.bfloat16)
        mine = jnp.where(own, jnp.broadcast_to(high[g:g + 1, :], (GROUP, SPAN)), -1).astype(jnp.int16)
        first = 0
        for out in refs[waits:]:
            tiles = out.shape[1] // SPAN
            left = jnp.concatenate([jnp.where(mine == jnp.int16(first + t), one, zero) for t in range(tiles)], 0)
            made = jnp.dot(left, right, preferred_element_type=jnp.float32).astype(jnp.bfloat16)
            for t in range(tiles):
                out[g * GROUP:(g + 1) * GROUP, t * SPAN:(t + 1) * SPAN] = made[t * GROUP:(t + 1) * GROUP]
            first += tiles

def pack_slots(slots_t, counts):
    deg, nodes = slots_t.shape
    groups = nodes // GROUP
    depth = SPAN // GROUP
    step = lax.broadcasted_iota(jnp.int32, (depth, nodes), 0)
    slots = jnp.pad(slots_t, ((0, depth - deg), (0, 0)), constant_values=-1)
    slots = jnp.where(step < counts[None, :], slots, -1)
    return slots.reshape(depth, groups, GROUP).transpose(1, 0, 2).reshape(groups, SPAN)


def incidence(slots, widths, after, batch=8):
    groups = slots.shape[0]
    nodes = groups * GROUP
    total = sum(widths)
    block = batch * GROUP
    return pl.pallas_call(
        functools.partial(incidence_kernel, len(after)),
        grid=(groups // batch,),
        in_specs=[pl.BlockSpec((batch, SPAN), lambda i: (i, 0))]
        + [pl.BlockSpec(memory_space=pl.ANY)] * len(after),
        out_specs=[pl.BlockSpec((block, w), lambda i: (i, 0)) for w in widths],
        out_shape=[jax.ShapeDtypeStruct((nodes, w), jnp.bfloat16) for w in widths],
        cost_estimate=pl.CostEstimate(flops=nodes, bytes_accessed=nodes, transcendentals=0),
        compiler_params=pltpu.CompilerParams(vmem_limit_bytes=56 << 20),
        name="incidence",
    )(slots, *after)


def mean_kernel(table_ref, weight_ref, start_ref, counts_ref, out_ref):
    rows = out_ref.shape[0]
    live = jnp.broadcast_to(counts_ref[...].astype(jnp.float32), (8, rows)).T[:, :1]
    total = start_ref[...] + jnp.dot(
        weight_ref[...], table_ref[...], preferred_element_type=jnp.float32
    )
    out_ref[...] = (total / live).astype(jnp.bfloat16)


def finish_mean(table, weight, start, counts, block=256):
    nodes, depth = weight.shape
    width = table.shape[1]
    return pl.pallas_call(
        mean_kernel,
        grid=(nodes // block,),
        in_specs=[
            pl.BlockSpec((depth, width), lambda i: (0, 0), pipeline_mode=pl.Buffered(1)),
            pl.BlockSpec((block, depth), lambda i: (i, 0)),
            pl.BlockSpec((block, width), lambda i: (i, 0)),
            pl.BlockSpec((1, block), lambda i: (0, i)),
        ],
        out_specs=pl.BlockSpec((block, width), lambda i: (i, 0)),
        out_shape=jax.ShapeDtypeStruct((nodes, width), jnp.bfloat16),
        cost_estimate=pl.CostEstimate(
            flops=2 * nodes * depth * width,
            bytes_accessed=2 * (nodes * depth + depth * width + 3 * nodes * width),
            transcendentals=0,
        ),
        compiler_params=pltpu.CompilerParams(vmem_limit_bytes=56 << 20),
        name="finish_mean",
    )(table, weight, start, counts.reshape(1, nodes))


def layer_kernel(core_ref, own, own_far, mean, mean_far, w_self, w_self_far, w_neigh, w_neigh_far,
                 cotangent_ref, out_ref, mine_ref, other_ref, total_ref):
    step = pl.program_id(0)

    def product(rows, weight):
        return jnp.dot(rows[...], weight[...], preferred_element_type=jnp.float32)

    pre = (product(own, w_self) + product(own_far, w_self_far)) + (
        product(mean, w_neigh) + product(mean_far, w_neigh_far)
    )
    scale = math.sqrt(2 / math.pi)
    square = pre * pre
    tanh = jnp.tanh(scale * (pre + 0.044715 * (square * pre)))
    half_up = 0.5 * (1.0 + tanh)
    out_ref[...] = (pre * half_up).astype(jnp.bfloat16)
    slope = half_up + 0.5 * pre * (1.0 - tanh * tanh) * (scale * (1.0 + 3 * 0.044715 * square))
    grad = (cotangent_ref[...].astype(jnp.float32) * slope).astype(jnp.bfloat16)
    part = jnp.concatenate(
        [
            lax.dot_general(
                grad, rows[...], (((0,), (0,)), ((), ())), preferred_element_type=jnp.float32
            )
            for rows in (own, mean, own_far, mean_far)
        ],
        1,
    )

    @pl.when(step == 0)
    def _():
        total_ref[...] = part

    @pl.when(step > 0)
    def _():
        total_ref[...] += part

    @pl.when(step == pl.num_programs(0) - 1)
    def _():
        total = total_ref[...].T.astype(jnp.bfloat16)
        mine_ref[...] = total[:mine_ref.shape[0]]
        other_ref[...] = total[mine_ref.shape[0]:]


def layer(core, own, own_far, mean, mean_far, w_self, w_self_far, w_neigh, w_neigh_far, cotangent, block=256):
    nodes, half = own.shape
    rows = pl.BlockSpec((block, half), lambda i, c: (i, 0))
    weight = pl.BlockSpec((half, half), lambda i, c: (0, c[0]), pipeline_mode=pl.Buffered(1))
    whole = pl.BlockSpec((2 * half, half), lambda i, c: (0, 0))
    return pl.pallas_call(
        layer_kernel,
        grid_spec=pltpu.PrefetchScalarGridSpec(
            num_scalar_prefetch=1,
            grid=(nodes // block,),
            in_specs=[rows] * 4 + [weight] * 4 + [rows],
            out_specs=[rows, whole, whole],
            scratch_shapes=[pltpu.VMEM((half, 4 * half), jnp.float32)],
        ),
        out_shape=[
            jax.ShapeDtypeStruct((nodes, half), jnp.bfloat16),
            jax.ShapeDtypeStruct((2 * half, half), jnp.bfloat16),
            jax.ShapeDtypeStruct((2 * half, half), jnp.bfloat16),
        ],
        cost_estimate=pl.CostEstimate(
            flops=16 * nodes * half * half, bytes_accessed=12 * nodes * half, transcendentals=nodes * half
        ),
        compiler_params=pltpu.CompilerParams(vmem_limit_bytes=24 << 20),
        name="layer",
    )(core, own, own_far, mean, mean_far, w_self, w_self_far, w_neigh, w_neigh_far, cotangent)


def swap(value):
    return lax.ppermute(value, "col", SWAP)


def shift(value, axis, offset):
    stride, size = LINES[axis]
    pairs = []
    for source in range(128):
        here = source // stride % size
        pairs.append((source, source + ((here + offset) % size - here) * stride))
    return lax.ppermute(value, "dom", pairs)


def nothing(value):
    return jnp.minimum(jnp.abs(value[0, 0]), 0)


def spread_z(block, picked):
    near = jnp.concatenate([block] + [shift(block, "z", -ahead) for ahead in (1, 2, 3)], 0)
    near = near + nothing(picked)
    return jnp.concatenate([near, shift(near, "z", -4)], 0)


def spread_y(line):
    return jnp.concatenate([line] + [shift(line, "y", -ahead) for ahead in (1, 2, 3)], 0)


def spread_x(plane, after, before, weight):
    middle = plane.shape[0] // 2
    zero = nothing(weight)
    return jnp.concatenate(
        [
            plane,
            after,
            shift(after[:middle] + zero, "x", -1),
            shift(before[middle:] + zero, "x", 1),
            before,
        ],
        0,
    )


def table_order(slots, nodes, hubs):
    here = lax.axis_index("dom")
    hub = slots - nodes
    owner = hub >> 5
    ahead_x = ((owner >> 5) - (here >> 5)) & 3
    ahead_y = ((owner >> 3) - (here >> 3)) & 3
    ahead_z = (owner - here) & 7
    moved = nodes + (((ahead_x * 4 + ahead_y) * 8 + ahead_z) << 5) + (hub & 31)
    return jnp.where((hub >= 0) & (hub < hubs), moved, slots)


def dot(left, right):
    return jnp.dot(left, right, preferred_element_type=jnp.float32)


def shards(features, cotangent, w_self, w_neigh, hub_rows, send_rows, neighbours, counts):
    parts = lax.axis_size("dom")
    nodes, half = features.shape
    core = lax.axis_index("col")
    features_far, w_self_far, w_neigh_far = swap(features), swap(w_self), swap(w_neigh)
    lanes = jnp.arange(nodes, dtype=jnp.int32)[None, :]

    def pick(rows):
        onehot = (rows[:, None] == lanes).astype(jnp.bfloat16)
        return dot(onehot, features).astype(jnp.bfloat16)

    outgoing = pick(send_rows.reshape(-1))
    plane = spread_y(spread_z(pick(hub_rows), outgoing))
    incoming = lax.all_to_all(
        outgoing.reshape(parts, -1, half), "dom", split_axis=0, concat_axis=0, tiled=True
    ).reshape(-1, half)
    hubs = parts * hub_rows.shape[0]
    slots = pack_slots(table_order(neighbours.T, nodes, hubs), counts)
    after, before = shift(plane, "x", -1), shift(plane, "x", 1)
    own_weight, hub_weight, far_weight = incidence(
        slots, (nodes, hubs, incoming.shape[0]), (plane, features_far, w_self_far, w_neigh_far)
    )
    table = spread_x(plane, after, before, own_weight)
    near_sum = dot(own_weight, features) + dot(hub_weight, table)
    neigh_mean = finish_mean(incoming, far_weight, near_sum, counts)
    mean_far = swap(neigh_mean)
    layer_out, mine, other = layer(
        core.astype(jnp.int32).reshape(1), features, features_far, neigh_mean, mean_far,
        w_self, w_self_far, w_neigh, w_neigh_far, cotangent,
    )
    partial = jnp.concatenate([mine, swap(other)], 0).reshape(parts, -1, half)
    pieces = lax.all_to_all(partial, "dom", split_axis=0, concat_axis=0, tiled=True)
    factor = 1.0 / math.sqrt(nodes * parts)
    piece = (pieces.astype(jnp.float32).sum(0) * factor).astype(jnp.bfloat16)
    sums = lax.all_to_all(
        jnp.broadcast_to(piece[None], (parts,) + piece.shape),
        "dom", split_axis=0, concat_axis=0, tiled=True,
    )
    sums = sums.reshape(2, 2, half, half).astype(jnp.float32)
    low = jnp.where(core == 0, sums[0], sums[1])
    high = jnp.where(core == 0, sums[1], sums[0])
    return (
        layer_out,
        jnp.concatenate([low[0], high[0]], 1),
        jnp.concatenate([low[1], high[1]], 1),
    )


def solution(mesh):
    placed = (
        P("dom", "col"),
        P("dom", "col"),
        P("col", None),
        P("col", None),
        P("dom"),
        P("dom", None, None),
        P("dom", None),
        P("dom"),
    )
    return jax.shard_map(
        shards,
        mesh=mesh,
        in_specs=placed,
        out_specs=(P("dom", "col"), P("col", None), P("col", None)),
        check_vma=False,
    )
```

```python
import functools
import math

import jax
import jax.numpy as jnp
from jax import lax
from jax.experimental import pallas as pl
from jax.experimental.pallas import tpu as pltpu
from jax.sharding import PartitionSpec as P

SWAP = [(0, 1), (1, 0)]
LINES = {"x": (32, 4), "y": (8, 4), "z": (1, 8)}
GROUP = 16
SPAN = 256


def incidence_kernel(waits, slots_ref, *refs):
    slots = slots_ref[...]
    low = (slots & (SPAN - 1)).astype(jnp.float32).T
    high = slots >> 8
    lane = lax.broadcasted_iota(jnp.int32, (SPAN, SPAN), 1).astype(jnp.float32)
    owner = lax.broadcasted_iota(jnp.int32, (GROUP, SPAN), 1) & (GROUP - 1)
    own = owner == lax.broadcasted_iota(jnp.int32, (GROUP, SPAN), 0)
    one = jnp.ones((GROUP, SPAN), jnp.bfloat16)
    zero = jnp.zeros((GROUP, SPAN), jnp.bfloat16)
    for g in range(slots.shape[0]):
        right = jnp.where(low[:, g:g + 1] == lane, 1.0, 0.0).astype(jnp.bfloat16)
        mine = jnp.where(own, jnp.broadcast_to(high[g:g + 1, :], (GROUP, SPAN)), -1).astype(jnp.int16)
        first = 0
        for out in refs[waits:]:
            tiles = out.shape[1] // SPAN
            left = jnp.concatenate([jnp.where(mine == jnp.int16(first + t), one, zero) for t in range(tiles)], 0)
            made = jnp.dot(left, right, preferred_element_type=jnp.float32).astype(jnp.bfloat16)
            for t in range(tiles):
                out[g * GROUP:(g + 1) * GROUP, t * SPAN:(t + 1) * SPAN] = made[t * GROUP:(t + 1) * GROUP]
            first += tiles

def pack_slots(slots_t, counts):
    deg, nodes = slots_t.shape
    groups = nodes // GROUP
    depth = SPAN // GROUP
    step = lax.broadcasted_iota(jnp.int32, (depth, nodes), 0)
    slots = jnp.pad(slots_t, ((0, depth - deg), (0, 0)), constant_values=-1)
    slots = jnp.where(step < counts[None, :], slots, -1)
    return slots.reshape(depth, groups, GROUP).transpose(1, 0, 2).reshape(groups, SPAN)


def incidence(slots, widths, after, batch=8):
    groups = slots.shape[0]
    nodes = groups * GROUP
    total = sum(widths)
    block = batch * GROUP
    return pl.pallas_call(
        functools.partial(incidence_kernel, len(after)),
        grid=(groups // batch,),
        in_specs=[pl.BlockSpec((batch, SPAN), lambda i: (i, 0))]
        + [pl.BlockSpec(memory_space=pl.ANY)] * len(after),
        out_specs=[pl.BlockSpec((block, w), lambda i: (i, 0)) for w in widths],
        out_shape=[jax.ShapeDtypeStruct((nodes, w), jnp.bfloat16) for w in widths],
        cost_estimate=pl.CostEstimate(flops=nodes, bytes_accessed=nodes, transcendentals=0),
        compiler_params=pltpu.CompilerParams(vmem_limit_bytes=56 << 20),
        name="incidence",
    )(slots, *after)


def layer_kernel(core_ref, own, own_far, mean, mean_far, w_self, w_self_far, w_neigh, w_neigh_far,
                 cotangent_ref, out_ref, mine_ref, other_ref, total_ref):
    step = pl.program_id(0)

    def product(rows, weight):
        return jnp.dot(rows[...], weight[...], preferred_element_type=jnp.float32)

    pre = (product(own, w_self) + product(own_far, w_self_far)) + (
        product(mean, w_neigh) + product(mean_far, w_neigh_far)
    )
    scale = math.sqrt(2 / math.pi)
    square = pre * pre
    tanh = jnp.tanh(scale * (pre + 0.044715 * (square * pre)))
    half_up = 0.5 * (1.0 + tanh)
    out_ref[...] = (pre * half_up).astype(jnp.bfloat16)
    slope = half_up + 0.5 * pre * (1.0 - tanh * tanh) * (scale * (1.0 + 3 * 0.044715 * square))
    grad = (cotangent_ref[...].astype(jnp.float32) * slope).astype(jnp.bfloat16)
    part = jnp.concatenate(
        [
            lax.dot_general(
                grad, rows[...], (((0,), (0,)), ((), ())), preferred_element_type=jnp.float32
            )
            for rows in (own, mean, own_far, mean_far)
        ],
        1,
    )

    @pl.when(step == 0)
    def _():
        total_ref[...] = part

    @pl.when(step > 0)
    def _():
        total_ref[...] += part

    @pl.when(step == pl.num_programs(0) - 1)
    def _():
        total = total_ref[...].T.astype(jnp.bfloat16)
        mine_ref[...] = total[:mine_ref.shape[0]]
        other_ref[...] = total[mine_ref.shape[0]:]


def layer(core, own, own_far, mean, mean_far, w_self, w_self_far, w_neigh, w_neigh_far, cotangent, block=256):
    nodes, half = own.shape
    rows = pl.BlockSpec((block, half), lambda i, c: (i, 0))
    weight = pl.BlockSpec((half, half), lambda i, c: (0, c[0]), pipeline_mode=pl.Buffered(1))
    whole = pl.BlockSpec((2 * half, half), lambda i, c: (0, 0))
    return pl.pallas_call(
        layer_kernel,
        grid_spec=pltpu.PrefetchScalarGridSpec(
            num_scalar_prefetch=1,
            grid=(nodes // block,),
            in_specs=[rows] * 4 + [weight] * 4 + [rows],
            out_specs=[rows, whole, whole],
            scratch_shapes=[pltpu.VMEM((half, 4 * half), jnp.float32)],
        ),
        out_shape=[
            jax.ShapeDtypeStruct((nodes, half), jnp.bfloat16),
            jax.ShapeDtypeStruct((2 * half, half), jnp.bfloat16),
            jax.ShapeDtypeStruct((2 * half, half), jnp.bfloat16),
        ],
        cost_estimate=pl.CostEstimate(
            flops=16 * nodes * half * half, bytes_accessed=12 * nodes * half, transcendentals=nodes * half
        ),
        compiler_params=pltpu.CompilerParams(vmem_limit_bytes=24 << 20),
        name="layer",
    )(core, own, own_far, mean, mean_far, w_self, w_self_far, w_neigh, w_neigh_far, cotangent)


def swap(value):
    return lax.ppermute(value, "col", SWAP)


def shift(value, axis, offset):
    stride, size = LINES[axis]
    pairs = []
    for source in range(128):
        here = source // stride % size
        pairs.append((source, source + ((here + offset) % size - here) * stride))
    return lax.ppermute(value, "dom", pairs)


def nothing(value):
    return jnp.minimum(jnp.abs(value[0, 0]), 0)


def exchange(blocks, axes):
    fixed = [(stride, size) for axis, (stride, size) in LINES.items() if axis not in axes]
    moving = [LINES[axis] for axis in axes]

    def spots(lines):
        found = [0]
        for stride, size in lines:
            found = [spot + step * stride for spot in found for step in range(size)]
        return found

    groups = [[base + spot for spot in spots(moving)] for base in spots(fixed)]
    return lax.all_to_all(
        blocks, "dom", split_axis=0, concat_axis=0, tiled=True, axis_index_groups=groups
    )


def share(block, axes):
    count = math.prod(LINES[axis][1] for axis in axes)
    return exchange(jnp.broadcast_to(block[None], (count,) + block.shape), axes)


def spread_y(line):
    return jnp.concatenate([line] + [shift(line, "y", -ahead) for ahead in (1, 2, 3)], 0)


def spread_x(plane, after, before, weight):
    middle = plane.shape[0] // 2
    zero = nothing(weight)
    return jnp.concatenate(
        [
            plane,
            after,
            shift(after[:middle] + zero, "x", -1),
            shift(before[middle:] + zero, "x", 1),
            before,
        ],
        0,
    )


def table_order(slots, nodes, hubs):
    here = lax.axis_index("dom")
    hub = slots - nodes
    owner = hub >> 5
    ahead_x = ((owner >> 5) - (here >> 5)) & 3
    ahead_y = ((owner >> 3) - (here >> 3)) & 3
    moved = nodes + ((ahead_x * 4 + ahead_y) << 8) + (hub & 255)
    return jnp.where((hub >= 0) & (hub < hubs), moved, slots)


def dot(left, right):
    return jnp.dot(left, right, preferred_element_type=jnp.float32)


def shards(features, cotangent, w_self, w_neigh, hub_rows, send_rows, neighbours, counts):
    parts = lax.axis_size("dom")
    nodes, half = features.shape
    core = lax.axis_index("col")
    features_far, w_self_far, w_neigh_far = swap(features), swap(w_self), swap(w_neigh)
    lanes = jnp.arange(nodes, dtype=jnp.int32)[None, :]

    def pick(rows):
        onehot = (rows[:, None] == lanes).astype(jnp.bfloat16)
        return dot(onehot, features).astype(jnp.bfloat16)

    outgoing = pick(send_rows.reshape(-1))
    plane = spread_y(share(pick(hub_rows), "z").reshape(-1, half))
    incoming = lax.all_to_all(
        outgoing.reshape(parts, -1, half), "dom", split_axis=0, concat_axis=0, tiled=True
    ).reshape(-1, half)
    hubs = parts * hub_rows.shape[0]
    slots = pack_slots(table_order(neighbours.T, nodes, hubs), counts)
    after, before = shift(plane, "x", -1), shift(plane, "x", 1)
    own_weight, hub_weight, far_weight = incidence(
        slots, (nodes, hubs, incoming.shape[0]), (plane, features_far, w_self_far, w_neigh_far)
    )
    table = spread_x(plane, after, before, own_weight)
    total = dot(own_weight, features) + dot(hub_weight, table) + dot(far_weight, incoming)
    neigh_mean = (total / counts[:, None].astype(jnp.float32)).astype(jnp.bfloat16)
    mean_far = swap(neigh_mean)
    layer_out, mine, other = layer(
        core.astype(jnp.int32).reshape(1), features, features_far, neigh_mean, mean_far,
        w_self, w_self_far, w_neigh, w_neigh_far, cotangent,
    )
    partial = jnp.concatenate([mine, swap(other)], 0).reshape(16, -1, half)

    def added(pieces):
        return pieces.astype(jnp.float32).sum(0)

    piece = added(exchange(partial, "xy")).astype(jnp.bfloat16)
    factor = 1.0 / math.sqrt(nodes * parts)
    piece = (added(share(piece, "z")) * factor).astype(jnp.bfloat16)
    sums = share(piece, "xy").reshape(2, 2, half, half).astype(jnp.float32)
    low = jnp.where(core == 0, sums[0], sums[1])
    high = jnp.where(core == 0, sums[1], sums[0])
    return (
        layer_out,
        jnp.concatenate([low[0], high[0]], 1),
        jnp.concatenate([low[1], high[1]], 1),
    )


def solution(mesh):
    placed = (
        P("dom", "col"),
        P("dom", "col"),
        P("col", None),
        P("col", None),
        P("dom"),
        P("dom", None, None),
        P("dom", None),
        P("dom"),
    )
    return jax.shard_map(
        shards,
        mesh=mesh,
        in_specs=placed,
        out_specs=(P("dom", "col"), P("col", None), P("col", None)),
        check_vma=False,
    )
```

```python
import functools
import math

import jax
import jax.numpy as jnp
from jax import lax
from jax.experimental import pallas as pl
from jax.experimental.pallas import tpu as pltpu
from jax.sharding import PartitionSpec as P

SWAP = [(0, 1), (1, 0)]
LINES = {"x": (32, 4), "y": (8, 4), "z": (1, 8)}
GROUP = 16
SPAN = 256


def incidence_kernel(waits, slots_ref, *refs):
    slots = slots_ref[...]
    low = (slots & (SPAN - 1)).astype(jnp.float32).T
    high = slots >> 8
    lane = lax.broadcasted_iota(jnp.int32, (SPAN, SPAN), 1).astype(jnp.float32)
    owner = lax.broadcasted_iota(jnp.int32, (GROUP, SPAN), 1) & (GROUP - 1)
    own = owner == lax.broadcasted_iota(jnp.int32, (GROUP, SPAN), 0)
    one = jnp.ones((GROUP, SPAN), jnp.bfloat16)
    zero = jnp.zeros((GROUP, SPAN), jnp.bfloat16)
    for g in range(slots.shape[0]):
        right = jnp.where(low[:, g:g + 1] == lane, 1.0, 0.0).astype(jnp.bfloat16)
        mine = jnp.where(own, jnp.broadcast_to(high[g:g + 1, :], (GROUP, SPAN)), -1).astype(jnp.int16)
        first = 0
        for out in refs[waits:]:
            tiles = out.shape[1] // SPAN
            left = jnp.concatenate([jnp.where(mine == jnp.int16(first + t), one, zero) for t in range(tiles)], 0)
            made = jnp.dot(left, right, preferred_element_type=jnp.float32).astype(jnp.bfloat16)
            for t in range(tiles):
                out[g * GROUP:(g + 1) * GROUP, t * SPAN:(t + 1) * SPAN] = made[t * GROUP:(t + 1) * GROUP]
            first += tiles

def pack_slots(slots_t, counts):
    deg, nodes = slots_t.shape
    groups = nodes // GROUP
    depth = SPAN // GROUP
    step = lax.broadcasted_iota(jnp.int32, (depth, nodes), 0)
    slots = jnp.pad(slots_t, ((0, depth - deg), (0, 0)), constant_values=-1)
    slots = jnp.where(step < counts[None, :], slots, -1)
    return slots.reshape(depth, groups, GROUP).transpose(1, 0, 2).reshape(groups, SPAN)


def incidence(slots, widths, after, batch=8):
    groups = slots.shape[0]
    nodes = groups * GROUP
    total = sum(widths)
    block = batch * GROUP
    return pl.pallas_call(
        functools.partial(incidence_kernel, len(after)),
        grid=(groups // batch,),
        in_specs=[pl.BlockSpec((batch, SPAN), lambda i: (i, 0))]
        + [pl.BlockSpec(memory_space=pl.ANY)] * len(after),
        out_specs=[pl.BlockSpec((block, w), lambda i: (i, 0)) for w in widths],
        out_shape=[jax.ShapeDtypeStruct((nodes, w), jnp.bfloat16) for w in widths],
        cost_estimate=pl.CostEstimate(flops=nodes, bytes_accessed=nodes, transcendentals=0),
        compiler_params=pltpu.CompilerParams(vmem_limit_bytes=56 << 20),
        name="incidence",
    )(slots, *after)


def layer_kernel(core_ref, own, own_far, mean, mean_far, w_self, w_self_far, w_neigh, w_neigh_far,
                 cotangent_ref, out_ref, mine_ref, other_ref, total_ref):
    step = pl.program_id(0)

    def product(rows, weight):
        return jnp.dot(rows[...], weight[...], preferred_element_type=jnp.float32)

    pre = (product(own, w_self) + product(own_far, w_self_far)) + (
        product(mean, w_neigh) + product(mean_far, w_neigh_far)
    )
    scale = math.sqrt(2 / math.pi)
    square = pre * pre
    tanh = jnp.tanh(scale * (pre + 0.044715 * (square * pre)))
    half_up = 0.5 * (1.0 + tanh)
    out_ref[...] = (pre * half_up).astype(jnp.bfloat16)
    slope = half_up + 0.5 * pre * (1.0 - tanh * tanh) * (scale * (1.0 + 3 * 0.044715 * square))
    grad = (cotangent_ref[...].astype(jnp.float32) * slope).astype(jnp.bfloat16)
    part = jnp.concatenate(
        [
            lax.dot_general(
                grad, rows[...], (((0,), (0,)), ((), ())), preferred_element_type=jnp.float32
            )
            for rows in (own, mean, own_far, mean_far)
        ],
        1,
    )

    @pl.when(step == 0)
    def _():
        total_ref[...] = part

    @pl.when(step > 0)
    def _():
        total_ref[...] += part

    @pl.when(step == pl.num_programs(0) - 1)
    def _():
        total = total_ref[...].T.astype(jnp.bfloat16)
        mine_ref[...] = total[:mine_ref.shape[0]]
        other_ref[...] = total[mine_ref.shape[0]:]


def layer(core, own, own_far, mean, mean_far, w_self, w_self_far, w_neigh, w_neigh_far, cotangent, block=256):
    nodes, half = own.shape
    rows = pl.BlockSpec((block, half), lambda i, c: (i, 0))
    weight = pl.BlockSpec((half, half), lambda i, c: (0, c[0]), pipeline_mode=pl.Buffered(1))
    whole = pl.BlockSpec((2 * half, half), lambda i, c: (0, 0))
    return pl.pallas_call(
        layer_kernel,
        grid_spec=pltpu.PrefetchScalarGridSpec(
            num_scalar_prefetch=1,
            grid=(nodes // block,),
            in_specs=[rows] * 4 + [weight] * 4 + [rows],
            out_specs=[rows, whole, whole],
            scratch_shapes=[pltpu.VMEM((half, 4 * half), jnp.float32)],
        ),
        out_shape=[
            jax.ShapeDtypeStruct((nodes, half), jnp.bfloat16),
            jax.ShapeDtypeStruct((2 * half, half), jnp.bfloat16),
            jax.ShapeDtypeStruct((2 * half, half), jnp.bfloat16),
        ],
        cost_estimate=pl.CostEstimate(
            flops=16 * nodes * half * half, bytes_accessed=12 * nodes * half, transcendentals=nodes * half
        ),
        compiler_params=pltpu.CompilerParams(vmem_limit_bytes=24 << 20),
        name="layer",
    )(core, own, own_far, mean, mean_far, w_self, w_self_far, w_neigh, w_neigh_far, cotangent)


def swap(value):
    return lax.ppermute(value, "col", SWAP)


def shift(value, axis, offset):
    stride, size = LINES[axis]
    pairs = []
    for source in range(128):
        here = source // stride % size
        pairs.append((source, source + ((here + offset) % size - here) * stride))
    return lax.ppermute(value, "dom", pairs)


def nothing(value):
    return jnp.minimum(jnp.abs(value[0, 0]), 0)


def exchange(blocks, axes):
    fixed = [(stride, size) for axis, (stride, size) in LINES.items() if axis not in axes]
    moving = [LINES[axis] for axis in axes]

    def spots(lines):
        found = [0]
        for stride, size in lines:
            found = [spot + step * stride for spot in found for step in range(size)]
        return found

    groups = [[base + spot for spot in spots(moving)] for base in spots(fixed)]
    return lax.all_to_all(
        blocks, "dom", split_axis=0, concat_axis=0, tiled=True, axis_index_groups=groups
    )


def share(block, axes):
    count = math.prod(LINES[axis][1] for axis in axes)
    return exchange(jnp.broadcast_to(block[None], (count,) + block.shape), axes)


def spread_y(line):
    return jnp.concatenate([line] + [shift(line, "y", -ahead) for ahead in (1, 2, 3)], 0)


def spread_x(plane, after, before, weight):
    middle = plane.shape[0] // 2
    zero = nothing(weight)
    return jnp.concatenate(
        [
            plane,
            after,
            shift(after[:middle] + zero, "x", -1),
            shift(before[middle:] + zero, "x", 1),
            before,
        ],
        0,
    )


def table_order(slots, nodes, hubs):
    here = lax.axis_index("dom")
    hub = slots - nodes
    owner = hub >> 5
    ahead_x = ((owner >> 5) - (here >> 5)) & 3
    ahead_y = ((owner >> 3) - (here >> 3)) & 3
    moved = nodes + ((ahead_x * 4 + ahead_y) << 8) + (hub & 255)
    return jnp.where((hub >= 0) & (hub < hubs), moved, slots)


def dot(left, right):
    return jnp.dot(left, right, preferred_element_type=jnp.float32)


def shards(features, cotangent, w_self, w_neigh, hub_rows, send_rows, neighbours, counts):
    parts = lax.axis_size("dom")
    nodes, half = features.shape
    core = lax.axis_index("col")
    features_far, w_self_far, w_neigh_far = swap(features), swap(w_self), swap(w_neigh)
    lanes = jnp.arange(nodes, dtype=jnp.int32)[None, :]

    def pick(rows):
        onehot = (rows[:, None] == lanes).astype(jnp.bfloat16)
        return dot(onehot, features).astype(jnp.bfloat16)

    line = share(pick(hub_rows), "z").reshape(-1, half)
    plane = spread_y(line)
    outgoing = pick(send_rows.reshape(-1) + nothing(line).astype(jnp.int32))
    incoming = lax.all_to_all(
        outgoing.reshape(parts, -1, half), "dom", split_axis=0, concat_axis=0, tiled=True
    ).reshape(-1, half)
    hubs = parts * hub_rows.shape[0]
    slots = pack_slots(table_order(neighbours.T, nodes, hubs), counts)
    after, before = shift(plane, "x", -1), shift(plane, "x", 1)
    own_weight, hub_weight, far_weight = incidence(
        slots, (nodes, hubs, incoming.shape[0]), (plane, features_far, w_self_far, w_neigh_far)
    )
    table = spread_x(plane, after, before, own_weight)
    near_sum = lax.optimization_barrier(dot(own_weight, features) + dot(hub_weight, table))
    total = near_sum + dot(far_weight, incoming)
    neigh_mean = (total / counts[:, None].astype(jnp.float32)).astype(jnp.bfloat16)
    mean_far = swap(neigh_mean)
    layer_out, mine, other = layer(
        core.astype(jnp.int32).reshape(1), features, features_far, neigh_mean, mean_far,
        w_self, w_self_far, w_neigh, w_neigh_far, cotangent,
    )
    partial = jnp.concatenate([mine, swap(other)], 0).reshape(16, -1, half)

    def added(pieces):
        return pieces.astype(jnp.float32).sum(0)

    piece = added(exchange(partial, "xy")).astype(jnp.bfloat16)
    factor = 1.0 / math.sqrt(nodes * parts)
    piece = (added(share(piece, "z")) * factor).astype(jnp.bfloat16)
    sums = share(piece, "xy").reshape(2, 2, half, half).astype(jnp.float32)
    low = jnp.where(core == 0, sums[0], sums[1])
    high = jnp.where(core == 0, sums[1], sums[0])
    return (
        layer_out,
        jnp.concatenate([low[0], high[0]], 1),
        jnp.concatenate([low[1], high[1]], 1),
    )


def solution(mesh):
    placed = (
        P("dom", "col"),
        P("dom", "col"),
        P("col", None),
        P("col", None),
        P("dom"),
        P("dom", None, None),
        P("dom", None),
        P("dom"),
    )
    return jax.shard_map(
        shards,
        mesh=mesh,
        in_specs=placed,
        out_specs=(P("dom", "col"), P("col", None), P("col", None)),
        check_vma=False,
    )
```

```python
import functools
import math

import jax
import jax.numpy as jnp
from jax import lax
from jax.experimental import pallas as pl
from jax.experimental.pallas import tpu as pltpu
from jax.sharding import PartitionSpec as P

SWAP = [(0, 1), (1, 0)]
LINES = {"x": (32, 4), "y": (8, 4), "z": (1, 8)}
GROUP = 16
SPAN = 256


def incidence_kernel(waits, slots_ref, *refs):
    *outs, token_ref = refs[waits:]
    token_ref[...] = jnp.zeros_like(token_ref)
    slots = slots_ref[...]
    low = (slots & (SPAN - 1)).astype(jnp.float32).T
    high = slots >> 8
    lane = lax.broadcasted_iota(jnp.int32, (SPAN, SPAN), 1).astype(jnp.float32)
    owner = lax.broadcasted_iota(jnp.int32, (GROUP, SPAN), 1) & (GROUP - 1)
    own = owner == lax.broadcasted_iota(jnp.int32, (GROUP, SPAN), 0)
    one = jnp.ones((GROUP, SPAN), jnp.bfloat16)
    zero = jnp.zeros((GROUP, SPAN), jnp.bfloat16)
    for g in range(slots.shape[0]):
        right = jnp.where(low[:, g:g + 1] == lane, 1.0, 0.0).astype(jnp.bfloat16)
        mine = jnp.where(own, jnp.broadcast_to(high[g:g + 1, :], (GROUP, SPAN)), -1).astype(jnp.int16)
        first = 0
        for out in outs:
            tiles = out.shape[1] // SPAN
            left = jnp.concatenate([jnp.where(mine == jnp.int16(first + t), one, zero) for t in range(tiles)], 0)
            made = jnp.dot(left, right, preferred_element_type=jnp.float32).astype(jnp.bfloat16)
            for t in range(tiles):
                out[g * GROUP:(g + 1) * GROUP, t * SPAN:(t + 1) * SPAN] = made[t * GROUP:(t + 1) * GROUP]
            first += tiles

def pack_slots(slots_t, counts):
    deg, nodes = slots_t.shape
    groups = nodes // GROUP
    depth = SPAN // GROUP
    step = lax.broadcasted_iota(jnp.int32, (depth, nodes), 0)
    slots = jnp.pad(slots_t, ((0, depth - deg), (0, 0)), constant_values=-1)
    slots = jnp.where(step < counts[None, :], slots, -1)
    return slots.reshape(depth, groups, GROUP).transpose(1, 0, 2).reshape(groups, SPAN)


def incidence(slots, widths, after, made=None, batch=8):
    groups = slots.shape[0]
    nodes = groups * GROUP
    total = sum(widths)
    block = batch * GROUP
    steps = groups // batch // 2
    first = 0 if made is None else steps
    made = made or ()
    waits = len(made) + len(after)
    *weights, token = pl.pallas_call(
        functools.partial(incidence_kernel, waits),
        grid=(steps,),
        in_specs=[pl.BlockSpec((batch, SPAN), lambda i: (i + first, 0))]
        + [pl.BlockSpec(memory_space=pl.ANY)] * waits,
        out_specs=[pl.BlockSpec((block, w), lambda i: (i + first, 0)) for w in widths]
        + [pl.BlockSpec((8, 128), lambda i: (0, 0))],
        out_shape=[jax.ShapeDtypeStruct((nodes, w), jnp.bfloat16) for w in widths]
        + [jax.ShapeDtypeStruct((8, 128), jnp.int32)],
        input_output_aliases={1 + i: i for i in range(len(made))},
        cost_estimate=pl.CostEstimate(
            flops=len(made) * 1000 * nodes * total // 3 + nodes, bytes_accessed=nodes, transcendentals=0
        ),
        compiler_params=pltpu.CompilerParams(vmem_limit_bytes=56 << 20),
        name="incidence",
    )(slots, *made, *after)
    return weights, token[0, 0]


def layer_kernel(core_ref, own, own_far, mean, mean_far, w_self, w_self_far, w_neigh, w_neigh_far,
                 cotangent_ref, out_ref, mine_ref, other_ref, total_ref):
    step = pl.program_id(0)

    def product(rows, weight):
        return jnp.dot(rows[...], weight[...], preferred_element_type=jnp.float32)

    pre = (product(own, w_self) + product(own_far, w_self_far)) + (
        product(mean, w_neigh) + product(mean_far, w_neigh_far)
    )
    scale = math.sqrt(2 / math.pi)
    square = pre * pre
    tanh = jnp.tanh(scale * (pre + 0.044715 * (square * pre)))
    half_up = 0.5 * (1.0 + tanh)
    out_ref[...] = (pre * half_up).astype(jnp.bfloat16)
    slope = half_up + 0.5 * pre * (1.0 - tanh * tanh) * (scale * (1.0 + 3 * 0.044715 * square))
    grad = (cotangent_ref[...].astype(jnp.float32) * slope).astype(jnp.bfloat16)
    part = jnp.concatenate(
        [
            lax.dot_general(
                grad, rows[...], (((0,), (0,)), ((), ())), preferred_element_type=jnp.float32
            )
            for rows in (own, mean, own_far, mean_far)
        ],
        1,
    )

    @pl.when(step == 0)
    def _():
        total_ref[...] = part

    @pl.when(step > 0)
    def _():
        total_ref[...] += part

    @pl.when(step == pl.num_programs(0) - 1)
    def _():
        total = total_ref[...].T.astype(jnp.bfloat16)
        mine_ref[...] = total[:mine_ref.shape[0]]
        other_ref[...] = total[mine_ref.shape[0]:]


def layer(core, own, own_far, mean, mean_far, w_self, w_self_far, w_neigh, w_neigh_far, cotangent, block=256):
    nodes, half = own.shape
    rows = pl.BlockSpec((block, half), lambda i, c: (i, 0))
    weight = pl.BlockSpec((half, half), lambda i, c: (0, c[0]), pipeline_mode=pl.Buffered(1))
    whole = pl.BlockSpec((2 * half, half), lambda i, c: (0, 0))
    return pl.pallas_call(
        layer_kernel,
        grid_spec=pltpu.PrefetchScalarGridSpec(
            num_scalar_prefetch=1,
            grid=(nodes // block,),
            in_specs=[rows] * 4 + [weight] * 4 + [rows],
            out_specs=[rows, whole, whole],
            scratch_shapes=[pltpu.VMEM((half, 4 * half), jnp.float32)],
        ),
        out_shape=[
            jax.ShapeDtypeStruct((nodes, half), jnp.bfloat16),
            jax.ShapeDtypeStruct((2 * half, half), jnp.bfloat16),
            jax.ShapeDtypeStruct((2 * half, half), jnp.bfloat16),
        ],
        cost_estimate=pl.CostEstimate(
            flops=16 * nodes * half * half, bytes_accessed=12 * nodes * half, transcendentals=nodes * half
        ),
        compiler_params=pltpu.CompilerParams(vmem_limit_bytes=24 << 20),
        name="layer",
    )(core, own, own_far, mean, mean_far, w_self, w_self_far, w_neigh, w_neigh_far, cotangent)


def swap(value):
    return lax.ppermute(value, "col", SWAP)


def shift(value, axis, offset):
    stride, size = LINES[axis]
    pairs = []
    for source in range(128):
        here = source // stride % size
        pairs.append((source, source + ((here + offset) % size - here) * stride))
    return lax.ppermute(value, "dom", pairs)


def nothing(value):
    return jnp.minimum(jnp.abs(value[0, 0]), 0)


def exchange(blocks, axes):
    fixed = [(stride, size) for axis, (stride, size) in LINES.items() if axis not in axes]
    moving = [LINES[axis] for axis in axes]

    def spots(lines):
        found = [0]
        for stride, size in lines:
            found = [spot + step * stride for spot in found for step in range(size)]
        return found

    groups = [[base + spot for spot in spots(moving)] for base in spots(fixed)]
    return lax.all_to_all(
        blocks, "dom", split_axis=0, concat_axis=0, tiled=True, axis_index_groups=groups
    )


def share(block, axes):
    count = math.prod(LINES[axis][1] for axis in axes)
    return exchange(jnp.broadcast_to(block[None], (count,) + block.shape), axes)


def spread_y(line):
    return jnp.concatenate([line] + [shift(line, "y", -ahead) for ahead in (1, 2, 3)], 0)


def spread_x(plane, after, before, token):
    middle = plane.shape[0] // 2
    zero = token.astype(plane.dtype)
    return jnp.concatenate(
        [
            plane,
            after,
            shift(after[:middle] + zero, "x", -1),
            shift(before[middle:] + zero, "x", 1),
            before,
        ],
        0,
    )


def table_order(slots, nodes, hubs):
    here = lax.axis_index("dom")
    hub = slots - nodes
    owner = hub >> 5
    ahead_x = ((owner >> 5) - (here >> 5)) & 3
    ahead_y = ((owner >> 3) - (here >> 3)) & 3
    moved = nodes + ((ahead_x * 4 + ahead_y) << 8) + (hub & 255)
    return jnp.where((hub >= 0) & (hub < hubs), moved, slots)


def dot(left, right):
    return jnp.dot(left, right, preferred_element_type=jnp.float32)


def shards(features, cotangent, w_self, w_neigh, hub_rows, send_rows, neighbours, counts):
    parts = lax.axis_size("dom")
    nodes, half = features.shape
    core = lax.axis_index("col")
    features_far, w_self_far, w_neigh_far = swap(features), swap(w_self), swap(w_neigh)
    lanes = jnp.arange(nodes, dtype=jnp.int32)[None, :]

    def pick(rows):
        onehot = (rows[:, None] == lanes).astype(jnp.bfloat16)
        return dot(onehot, features).astype(jnp.bfloat16)

    hubs = parts * hub_rows.shape[0]
    slots = pack_slots(table_order(neighbours.T, nodes, hubs), counts)
    widths = (nodes, hubs, parts * send_rows.shape[2])
    made, token = incidence(slots, widths, ())
    line = share(pick(hub_rows), "z").reshape(-1, half)
    plane = spread_y(line)
    outgoing = pick(send_rows.reshape(-1) + (nothing(line).astype(jnp.int32) + token))
    incoming = lax.all_to_all(
        outgoing.reshape(parts, -1, half), "dom", split_axis=0, concat_axis=0, tiled=True
    ).reshape(-1, half)
    after, before = shift(plane, "x", -1), shift(plane, "x", 1)
    (own_weight, hub_weight, far_weight), token = incidence(
        slots, widths, (plane, features_far, w_self_far, w_neigh_far), made
    )
    table = spread_x(plane, after, before, token)
    own_sum = lax.optimization_barrier(dot(own_weight, features))
    near_sum = lax.optimization_barrier(own_sum + dot(hub_weight, table))
    total = near_sum + dot(far_weight, incoming)
    neigh_mean = (total / counts[:, None].astype(jnp.float32)).astype(jnp.bfloat16)
    mean_far = swap(neigh_mean)
    layer_out, mine, other = layer(
        core.astype(jnp.int32).reshape(1), features, features_far, neigh_mean, mean_far,
        w_self, w_self_far, w_neigh, w_neigh_far, cotangent,
    )
    partial = jnp.concatenate([mine, swap(other)], 0).reshape(16, -1, half)

    def added(pieces):
        return pieces.astype(jnp.float32).sum(0)

    piece = added(exchange(partial, "xy")).astype(jnp.bfloat16)
    factor = 1.0 / math.sqrt(nodes * parts)
    piece = (added(share(piece, "z")) * factor).astype(jnp.bfloat16)
    sums = share(piece, "xy").reshape(2, 2, half, half).astype(jnp.float32)
    low = jnp.where(core == 0, sums[0], sums[1])
    high = jnp.where(core == 0, sums[1], sums[0])
    return (
        layer_out,
        jnp.concatenate([low[0], high[0]], 1),
        jnp.concatenate([low[1], high[1]], 1),
    )


def solution(mesh):
    placed = (
        P("dom", "col"),
        P("dom", "col"),
        P("col", None),
        P("col", None),
        P("dom"),
        P("dom", None, None),
        P("dom", None),
        P("dom"),
    )
    return jax.shard_map(
        shards,
        mesh=mesh,
        in_specs=placed,
        out_specs=(P("dom", "col"), P("col", None), P("col", None)),
        check_vma=False,
    )
```

```python
import functools
import math

import jax
import jax.numpy as jnp
from jax import lax
from jax.experimental import pallas as pl
from jax.experimental.pallas import tpu as pltpu
from jax.sharding import PartitionSpec as P

SWAP = [(0, 1), (1, 0)]
LINES = {"x": (32, 4), "y": (8, 4), "z": (1, 8)}
GROUP = 16
SPAN = 256


def incidence_kernel(waits, slots_ref, *refs):
    *outs, token_ref = refs[waits:]
    token_ref[...] = jnp.zeros_like(token_ref)
    slots = slots_ref[...]
    low = (slots & (SPAN - 1)).astype(jnp.float32).T
    high = slots >> 8
    lane = lax.broadcasted_iota(jnp.int32, (SPAN, SPAN), 1).astype(jnp.float32)
    owner = lax.broadcasted_iota(jnp.int32, (GROUP, SPAN), 1) & (GROUP - 1)
    own = owner == lax.broadcasted_iota(jnp.int32, (GROUP, SPAN), 0)
    one = jnp.ones((GROUP, SPAN), jnp.bfloat16)
    zero = jnp.zeros((GROUP, SPAN), jnp.bfloat16)
    for g in range(slots.shape[0]):
        right = jnp.where(low[:, g:g + 1] == lane, 1.0, 0.0).astype(jnp.bfloat16)
        mine = jnp.where(own, jnp.broadcast_to(high[g:g + 1, :], (GROUP, SPAN)), -1).astype(jnp.int16)
        first = 0
        for out in outs:
            tiles = out.shape[1] // SPAN
            left = jnp.concatenate([jnp.where(mine == jnp.int16(first + t), one, zero) for t in range(tiles)], 0)
            made = jnp.dot(left, right, preferred_element_type=jnp.float32).astype(jnp.bfloat16)
            for t in range(tiles):
                out[g * GROUP:(g + 1) * GROUP, t * SPAN:(t + 1) * SPAN] = made[t * GROUP:(t + 1) * GROUP]
            first += tiles

def pack_slots(slots_t, counts):
    deg, nodes = slots_t.shape
    groups = nodes // GROUP
    depth = SPAN // GROUP
    step = lax.broadcasted_iota(jnp.int32, (depth, nodes), 0)
    slots = jnp.pad(slots_t, ((0, depth - deg), (0, 0)), constant_values=-1)
    slots = jnp.where(step < counts[None, :], slots, -1)
    return slots.reshape(depth, groups, GROUP).transpose(1, 0, 2).reshape(groups, SPAN)


def incidence(slots, widths, after, made=None, batch=8):
    groups = slots.shape[0]
    nodes = groups * GROUP
    total = sum(widths)
    block = batch * GROUP
    steps = groups // batch // 2
    first = 0 if made is None else steps
    made = made or ()
    waits = len(made) + len(after)
    *weights, token = pl.pallas_call(
        functools.partial(incidence_kernel, waits),
        grid=(steps,),
        in_specs=[pl.BlockSpec((batch, SPAN), lambda i: (i + first, 0))]
        + [pl.BlockSpec(memory_space=pl.ANY)] * waits,
        out_specs=[pl.BlockSpec((block, w), lambda i: (i + first, 0)) for w in widths]
        + [pl.BlockSpec((8, 128), lambda i: (0, 0))],
        out_shape=[jax.ShapeDtypeStruct((nodes, w), jnp.bfloat16) for w in widths]
        + [jax.ShapeDtypeStruct((8, 128), jnp.int32)],
        input_output_aliases={1 + i: i for i in range(len(made))},
        cost_estimate=pl.CostEstimate(
            flops=nodes, bytes_accessed=nodes, transcendentals=0
        ),
        compiler_params=pltpu.CompilerParams(vmem_limit_bytes=56 << 20),
        name="incidence",
    )(slots, *made, *after)
    return weights, token[0, 0]


def layer_kernel(core_ref, own, own_far, mean, mean_far, w_self, w_self_far, w_neigh, w_neigh_far,
                 cotangent_ref, out_ref, mine_ref, other_ref, total_ref):
    step = pl.program_id(0)

    def product(rows, weight):
        return jnp.dot(rows[...], weight[...], preferred_element_type=jnp.float32)

    pre = (product(own, w_self) + product(own_far, w_self_far)) + (
        product(mean, w_neigh) + product(mean_far, w_neigh_far)
    )
    scale = math.sqrt(2 / math.pi)
    square = pre * pre
    tanh = jnp.tanh(scale * (pre + 0.044715 * (square * pre)))
    half_up = 0.5 * (1.0 + tanh)
    out_ref[...] = (pre * half_up).astype(jnp.bfloat16)
    slope = half_up + 0.5 * pre * (1.0 - tanh * tanh) * (scale * (1.0 + 3 * 0.044715 * square))
    grad = (cotangent_ref[...].astype(jnp.float32) * slope).astype(jnp.bfloat16)
    part = jnp.concatenate(
        [
            lax.dot_general(
                grad, rows[...], (((0,), (0,)), ((), ())), preferred_element_type=jnp.float32
            )
            for rows in (own, mean, own_far, mean_far)
        ],
        1,
    )

    @pl.when(step == 0)
    def _():
        total_ref[...] = part

    @pl.when(step > 0)
    def _():
        total_ref[...] += part

    @pl.when(step == pl.num_programs(0) - 1)
    def _():
        total = total_ref[...].T.astype(jnp.bfloat16)
        mine_ref[...] = total[:mine_ref.shape[0]]
        other_ref[...] = total[mine_ref.shape[0]:]


def layer(core, own, own_far, mean, mean_far, w_self, w_neigh, weights_far, cotangent, block=256):
    nodes, half = own.shape
    rows = pl.BlockSpec((block, half), lambda i, c: (i, 0))

    def weight(place):
        return pl.BlockSpec((half, half), lambda i, c: (place, c[0]), pipeline_mode=pl.Buffered(1))

    whole = pl.BlockSpec((2 * half, half), lambda i, c: (0, 0))
    return pl.pallas_call(
        layer_kernel,
        grid_spec=pltpu.PrefetchScalarGridSpec(
            num_scalar_prefetch=1,
            grid=(nodes // block,),
            in_specs=[rows] * 4 + [weight(0), weight(0), weight(0), weight(1), rows],
            out_specs=[rows, whole, whole],
            scratch_shapes=[pltpu.VMEM((half, 4 * half), jnp.float32)],
        ),
        out_shape=[
            jax.ShapeDtypeStruct((nodes, half), jnp.bfloat16),
            jax.ShapeDtypeStruct((2 * half, half), jnp.bfloat16),
            jax.ShapeDtypeStruct((2 * half, half), jnp.bfloat16),
        ],
        cost_estimate=pl.CostEstimate(
            flops=16 * nodes * half * half, bytes_accessed=12 * nodes * half, transcendentals=nodes * half
        ),
        compiler_params=pltpu.CompilerParams(vmem_limit_bytes=24 << 20),
        name="layer",
    )(core, own, own_far, mean, mean_far, w_self, weights_far, w_neigh, weights_far, cotangent)


def swap(value):
    return lax.ppermute(value, "col", SWAP)


def shift(value, axis, offset):
    stride, size = LINES[axis]
    pairs = []
    for source in range(128):
        here = source // stride % size
        pairs.append((source, source + ((here + offset) % size - here) * stride))
    return lax.ppermute(value, "dom", pairs)


def exchange(blocks, axes):
    fixed = [(stride, size) for axis, (stride, size) in LINES.items() if axis not in axes]
    moving = [LINES[axis] for axis in axes]

    def spots(lines):
        found = [0]
        for stride, size in lines:
            found = [spot + step * stride for spot in found for step in range(size)]
        return found

    groups = [[base + spot for spot in spots(moving)] for base in spots(fixed)]
    return lax.all_to_all(
        blocks, "dom", split_axis=0, concat_axis=0, tiled=True, axis_index_groups=groups
    )


def share(block, axes):
    count = math.prod(LINES[axis][1] for axis in axes)
    return exchange(jnp.broadcast_to(block[None], (count,) + block.shape), axes)


def spread_y(line, token):
    rows = [line] + [shift(line, "y", -ahead) for ahead in (1, 2, 3)]
    return jnp.concatenate(rows, 0) + token.astype(line.dtype)


def opposite(after, before, token):
    middle = after.shape[0] // 2
    zero = token.astype(after.dtype)
    return jnp.concatenate(
        [shift(after[:middle] + zero, "x", -1), shift(before[middle:] + zero, "x", 1)], 0
    )


def table_order(slots, nodes, hubs):
    here = lax.axis_index("dom")
    hub = slots - nodes
    owner = hub >> 5
    ahead_x = ((owner >> 5) - (here >> 5)) & 3
    ahead_x = ahead_x ^ (ahead_x >> 1)
    ahead_y = ((owner >> 3) - (here >> 3)) & 3
    moved = nodes + ((ahead_x * 4 + ahead_y) << 8) + (hub & 255)
    return jnp.where((hub >= 0) & (hub < hubs), moved, slots)


def dot(left, right):
    return jnp.dot(left, right, preferred_element_type=jnp.float32)


def shards(features, cotangent, w_self, w_neigh, hub_rows, send_rows, neighbours, counts):
    parts = lax.axis_size("dom")
    nodes, half = features.shape
    core = lax.axis_index("col")
    features_far, weights_far = swap(features), swap(jnp.concatenate([w_self, w_neigh], 0))
    lanes = jnp.arange(nodes, dtype=jnp.int32)[None, :]

    def pick(rows):
        onehot = (rows[:, None] == lanes).astype(jnp.bfloat16)
        return dot(onehot, features).astype(jnp.bfloat16)

    hubs = parts * hub_rows.shape[0]
    slots = pack_slots(table_order(neighbours.T, nodes, hubs), counts)
    widths = (nodes,) + (hubs // 4,) * 4 + (parts * send_rows.shape[2],)
    outgoing = pick(send_rows.reshape(-1))
    incoming = lax.all_to_all(
        outgoing.reshape(parts, -1, half), "dom", split_axis=0, concat_axis=0, tiled=True
    ).reshape(-1, half)
    line = share(pick(hub_rows), "z").reshape(-1, half)
    made, token = incidence(slots, widths, (line,))
    plane = spread_y(line, token)
    after, before = shift(plane, "x", -1), shift(plane, "x", 1)
    weights, token = incidence(slots, widths, (plane, features_far, weights_far), made)
    far = opposite(after, before, token)
    fence = lax.optimization_barrier
    total = fence(dot(weights[0], features))
    for weight, rows in zip(weights[1:4], (plane, after, before)):
        total = fence(total + dot(weight, rows))
    total = fence(total + dot(weights[4], far))
    total = total + dot(weights[5], incoming)
    neigh_mean = (total / counts[:, None].astype(jnp.float32)).astype(jnp.bfloat16)
    mean_far = swap(neigh_mean)
    layer_out, mine, other = layer(
        core.astype(jnp.int32).reshape(1), features, features_far, neigh_mean, mean_far,
        w_self, w_neigh, weights_far, cotangent,
    )
    partial = jnp.concatenate([mine, swap(other)], 0).reshape(16, -1, half)

    def added(pieces):
        return pieces.astype(jnp.float32).sum(0)

    piece = added(exchange(partial, "xy")).astype(jnp.bfloat16)
    factor = 1.0 / math.sqrt(nodes * parts)
    piece = (added(share(piece, "z")) * factor).astype(jnp.bfloat16)
    sums = share(piece, "xy").reshape(2, 2, half, half).astype(jnp.float32)
    low = jnp.where(core == 0, sums[0], sums[1])
    high = jnp.where(core == 0, sums[1], sums[0])
    return (
        layer_out,
        jnp.concatenate([low[0], high[0]], 1),
        jnp.concatenate([low[1], high[1]], 1),
    )


def solution(mesh):
    placed = (
        P("dom", "col"),
        P("dom", "col"),
        P("col", None),
        P("col", None),
        P("dom"),
        P("dom", None, None),
        P("dom", None),
        P("dom"),
    )
    return jax.shard_map(
        shards,
        mesh=mesh,
        in_specs=placed,
        out_specs=(P("dom", "col"), P("col", None), P("col", None)),
        check_vma=False,
    )
```

```python
import functools
import math

import jax
import jax.numpy as jnp
from jax import lax
from jax.experimental import pallas as pl
from jax.experimental.pallas import tpu as pltpu
from jax.sharding import PartitionSpec as P

SWAP = [(0, 1), (1, 0)]
LINES = {"x": (32, 4), "y": (8, 4), "z": (1, 8)}
GROUP = 16
SPAN = 256


def incidence_kernel(waits, slots_ref, *refs):
    *outs, token_ref = refs[waits:]
    token_ref[...] = jnp.zeros_like(token_ref)
    slots = slots_ref[...]
    low = (slots & (SPAN - 1)).astype(jnp.float32).T
    high = slots >> 8
    lane = lax.broadcasted_iota(jnp.int32, (SPAN, SPAN), 1).astype(jnp.float32)
    owner = lax.broadcasted_iota(jnp.int32, (GROUP, SPAN), 1) & (GROUP - 1)
    own = owner == lax.broadcasted_iota(jnp.int32, (GROUP, SPAN), 0)
    one = jnp.ones((GROUP, SPAN), jnp.bfloat16)
    zero = jnp.zeros((GROUP, SPAN), jnp.bfloat16)
    for g in range(slots.shape[0]):
        right = jnp.where(low[:, g:g + 1] == lane, 1.0, 0.0).astype(jnp.bfloat16)
        mine = jnp.where(own, jnp.broadcast_to(high[g:g + 1, :], (GROUP, SPAN)), -1).astype(jnp.int16)
        first = 0
        for out in outs:
            tiles = out.shape[1] // SPAN
            left = jnp.concatenate([jnp.where(mine == jnp.int16(first + t), one, zero) for t in range(tiles)], 0)
            made = jnp.dot(left, right, preferred_element_type=jnp.float32).astype(jnp.bfloat16)
            for t in range(tiles):
                out[g * GROUP:(g + 1) * GROUP, t * SPAN:(t + 1) * SPAN] = made[t * GROUP:(t + 1) * GROUP]
            first += tiles

def pack_slots(slots_t, counts):
    deg, nodes = slots_t.shape
    groups = nodes // GROUP
    depth = SPAN // GROUP
    step = lax.broadcasted_iota(jnp.int32, (depth, nodes), 0)
    slots = jnp.pad(slots_t, ((0, depth - deg), (0, 0)), constant_values=-1)
    slots = jnp.where(step < counts[None, :], slots, -1)
    return slots.reshape(depth, groups, GROUP).transpose(1, 0, 2).reshape(groups, SPAN)


def incidence(slots, widths, after, batch=8):
    groups = slots.shape[0]
    nodes = groups * GROUP
    block = batch * GROUP
    *weights, token = pl.pallas_call(
        functools.partial(incidence_kernel, len(after)),
        grid=(groups // batch,),
        in_specs=[pl.BlockSpec((batch, SPAN), lambda i: (i, 0))]
        + [pl.BlockSpec(memory_space=pl.ANY)] * len(after),
        out_specs=[pl.BlockSpec((block, w), lambda i: (i, 0)) for w in widths]
        + [pl.BlockSpec((8, 128), lambda i: (0, 0))],
        out_shape=[jax.ShapeDtypeStruct((nodes, w), jnp.bfloat16) for w in widths]
        + [jax.ShapeDtypeStruct((8, 128), jnp.int32)],
        cost_estimate=pl.CostEstimate(
            flops=nodes, bytes_accessed=nodes, transcendentals=0
        ),
        compiler_params=pltpu.CompilerParams(vmem_limit_bytes=56 << 20),
        name="incidence",
    )(slots, *after)
    return weights, token[0, 0]


def layer_kernel(core_ref, own, own_far, mean, mean_far, w_self, w_self_far, w_neigh, w_neigh_far,
                 cotangent_ref, out_ref, mine_ref, other_ref, total_ref):
    step = pl.program_id(0)

    def product(rows, weight):
        return jnp.dot(rows[...], weight[...], preferred_element_type=jnp.float32)

    pre = (product(own, w_self) + product(own_far, w_self_far)) + (
        product(mean, w_neigh) + product(mean_far, w_neigh_far)
    )
    scale = math.sqrt(2 / math.pi)
    square = pre * pre
    tanh = jnp.tanh(scale * (pre + 0.044715 * (square * pre)))
    half_up = 0.5 * (1.0 + tanh)
    out_ref[...] = (pre * half_up).astype(jnp.bfloat16)
    slope = half_up + 0.5 * pre * (1.0 - tanh * tanh) * (scale * (1.0 + 3 * 0.044715 * square))
    grad = (cotangent_ref[...].astype(jnp.float32) * slope).astype(jnp.bfloat16)
    part = jnp.concatenate(
        [
            lax.dot_general(
                grad, rows[...], (((0,), (0,)), ((), ())), preferred_element_type=jnp.float32
            )
            for rows in (own, mean, own_far, mean_far)
        ],
        1,
    )

    @pl.when(step == 0)
    def _():
        total_ref[...] = part

    @pl.when(step > 0)
    def _():
        total_ref[...] += part

    @pl.when(step == pl.num_programs(0) - 1)
    def _():
        total = total_ref[...].T.astype(jnp.bfloat16)
        mine_ref[...] = total[:mine_ref.shape[0]]
        other_ref[...] = total[mine_ref.shape[0]:]


def layer(core, own, own_far, mean, mean_far, w_self, w_neigh, weights_far, cotangent, block=256):
    nodes, half = own.shape
    rows = pl.BlockSpec((block, half), lambda i, c: (i, 0))

    def weight(place):
        return pl.BlockSpec((half, half), lambda i, c: (place, c[0]), pipeline_mode=pl.Buffered(1))

    whole = pl.BlockSpec((2 * half, half), lambda i, c: (0, 0))
    return pl.pallas_call(
        layer_kernel,
        grid_spec=pltpu.PrefetchScalarGridSpec(
            num_scalar_prefetch=1,
            grid=(nodes // block,),
            in_specs=[rows] * 4 + [weight(0), weight(0), weight(0), weight(1), rows],
            out_specs=[rows, whole, whole],
            scratch_shapes=[pltpu.VMEM((half, 4 * half), jnp.float32)],
        ),
        out_shape=[
            jax.ShapeDtypeStruct((nodes, half), jnp.bfloat16),
            jax.ShapeDtypeStruct((2 * half, half), jnp.bfloat16),
            jax.ShapeDtypeStruct((2 * half, half), jnp.bfloat16),
        ],
        cost_estimate=pl.CostEstimate(
            flops=16 * nodes * half * half, bytes_accessed=12 * nodes * half, transcendentals=nodes * half
        ),
        compiler_params=pltpu.CompilerParams(vmem_limit_bytes=24 << 20),
        name="layer",
    )(core, own, own_far, mean, mean_far, w_self, weights_far, w_neigh, weights_far, cotangent)


def swap(value):
    return lax.ppermute(value, "col", SWAP)


def shift(value, axis, offset):
    stride, size = LINES[axis]
    pairs = []
    for source in range(128):
        here = source // stride % size
        pairs.append((source, source + ((here + offset) % size - here) * stride))
    return lax.ppermute(value, "dom", pairs)


def exchange(blocks, axes):
    fixed = [(stride, size) for axis, (stride, size) in LINES.items() if axis not in axes]
    moving = [LINES[axis] for axis in axes]

    def spots(lines):
        found = [0]
        for stride, size in lines:
            found = [spot + step * stride for spot in found for step in range(size)]
        return found

    groups = [[base + spot for spot in spots(moving)] for base in spots(fixed)]
    return lax.all_to_all(
        blocks, "dom", split_axis=0, concat_axis=0, tiled=True, axis_index_groups=groups
    )


def share(block, axes):
    count = math.prod(LINES[axis][1] for axis in axes)
    return exchange(jnp.broadcast_to(block[None], (count,) + block.shape), axes)


def spread_y(line, token):
    rows = [line] + [shift(line, "y", -ahead) for ahead in (1, 2, 3)]
    return jnp.concatenate(rows, 0) + token.astype(line.dtype)


def opposite(after, before, token):
    middle = after.shape[0] // 2
    zero = token.astype(after.dtype)
    return jnp.concatenate(
        [shift(after[:middle] + zero, "x", -1), shift(before[middle:] + zero, "x", 1)], 0
    )


def table_order(slots, nodes, hubs):
    here = lax.axis_index("dom")
    hub = slots - nodes
    owner = hub >> 5
    ahead_x = ((owner >> 5) - (here >> 5)) & 3
    ahead_x = ahead_x ^ (ahead_x >> 1)
    ahead_y = ((owner >> 3) - (here >> 3)) & 3
    moved = nodes + ((ahead_x * 4 + ahead_y) << 8) + (hub & 255)
    return jnp.where((hub >= 0) & (hub < hubs), moved, slots)


def dot(left, right):
    return jnp.dot(left, right, preferred_element_type=jnp.float32)


def shards(features, cotangent, w_self, w_neigh, hub_rows, send_rows, neighbours, counts):
    parts = lax.axis_size("dom")
    nodes, half = features.shape
    core = lax.axis_index("col")
    features_far, weights_far = swap(features), swap(jnp.concatenate([w_self, w_neigh], 0))
    lanes = jnp.arange(nodes, dtype=jnp.int32)[None, :]

    def pick(rows):
        onehot = (rows[:, None] == lanes).astype(jnp.bfloat16)
        return dot(onehot, features).astype(jnp.bfloat16)

    hubs = parts * hub_rows.shape[0]
    slots = pack_slots(table_order(neighbours.T, nodes, hubs), counts)
    widths = (nodes,) + (hubs // 4,) * 4 + (parts * send_rows.shape[2],)
    outgoing = pick(send_rows.reshape(-1))
    incoming = lax.all_to_all(
        outgoing.reshape(parts, -1, half), "dom", split_axis=0, concat_axis=0, tiled=True
    ).reshape(-1, half)
    line = share(pick(hub_rows), "z").reshape(-1, half)
    plane = spread_y(line, jnp.minimum(jnp.abs(slots[0, 0]), 0))
    after, before = shift(plane, "x", -1), shift(plane, "x", 1)
    weights, token = incidence(slots, widths, (plane, features_far, weights_far))
    far = opposite(after, before, token)
    fence = lax.optimization_barrier
    total = fence(dot(weights[0], features))
    for weight, rows in zip(weights[1:4], (plane, after, before)):
        total = fence(total + dot(weight, rows))
    total = fence(total + dot(weights[4], far))
    total = total + dot(weights[5], incoming)
    neigh_mean = (total / counts[:, None].astype(jnp.float32)).astype(jnp.bfloat16)
    mean_far = swap(neigh_mean)
    layer_out, mine, other = layer(
        core.astype(jnp.int32).reshape(1), features, features_far, neigh_mean, mean_far,
        w_self, w_neigh, weights_far, cotangent,
    )
    partial = jnp.concatenate([mine, swap(other)], 0).reshape(16, -1, half)

    def added(pieces):
        return pieces.astype(jnp.float32).sum(0)

    piece = added(exchange(partial, "xy")).astype(jnp.bfloat16)
    factor = 1.0 / math.sqrt(nodes * parts)
    piece = (added(share(piece, "z")) * factor).astype(jnp.bfloat16)
    sums = share(piece, "xy").reshape(2, 2, half, half).astype(jnp.float32)
    low = jnp.where(core == 0, sums[0], sums[1])
    high = jnp.where(core == 0, sums[1], sums[0])
    return (
        layer_out,
        jnp.concatenate([low[0], high[0]], 1),
        jnp.concatenate([low[1], high[1]], 1),
    )


def solution(mesh):
    placed = (
        P("dom", "col"),
        P("dom", "col"),
        P("col", None),
        P("col", None),
        P("dom"),
        P("dom", None, None),
        P("dom", None),
        P("dom"),
    )
    return jax.shard_map(
        shards,
        mesh=mesh,
        in_specs=placed,
        out_specs=(P("dom", "col"), P("col", None), P("col", None)),
        check_vma=False,
    )
```

```python
import functools
import math

import jax
import jax.numpy as jnp
from jax import lax
from jax.experimental import pallas as pl
from jax.experimental.pallas import tpu as pltpu
from jax.sharding import PartitionSpec as P

SWAP = [(0, 1), (1, 0)]
LINES = {"x": (32, 4), "y": (8, 4), "z": (1, 8)}
GROUP = 16
SPAN = 256


def incidence_kernel(waits, slots_ref, *refs):
    *outs, token_ref = refs[waits:]
    token_ref[...] = jnp.zeros_like(token_ref)
    slots = slots_ref[...]
    low = (slots & (SPAN - 1)).astype(jnp.float32).T
    high = slots >> 8
    lane = lax.broadcasted_iota(jnp.int32, (SPAN, SPAN), 1).astype(jnp.float32)
    owner = lax.broadcasted_iota(jnp.int32, (GROUP, SPAN), 1) & (GROUP - 1)
    own = owner == lax.broadcasted_iota(jnp.int32, (GROUP, SPAN), 0)
    one = jnp.ones((GROUP, SPAN), jnp.bfloat16)
    zero = jnp.zeros((GROUP, SPAN), jnp.bfloat16)
    for g in range(slots.shape[0]):
        right = jnp.where(low[:, g:g + 1] == lane, 1.0, 0.0).astype(jnp.bfloat16)
        mine = jnp.where(own, jnp.broadcast_to(high[g:g + 1, :], (GROUP, SPAN)), -1).astype(jnp.int16)
        first = 0
        for out in outs:
            tiles = out.shape[1] // SPAN
            left = jnp.concatenate([jnp.where(mine == jnp.int16(first + t), one, zero) for t in range(tiles)], 0)
            made = jnp.dot(left, right, preferred_element_type=jnp.float32).astype(jnp.bfloat16)
            for t in range(tiles):
                out[g * GROUP:(g + 1) * GROUP, t * SPAN:(t + 1) * SPAN] = made[t * GROUP:(t + 1) * GROUP]
            first += tiles

def pack_slots(slots_t, counts):
    deg, nodes = slots_t.shape
    groups = nodes // GROUP
    depth = SPAN // GROUP
    step = lax.broadcasted_iota(jnp.int32, (depth, nodes), 0)
    slots = jnp.pad(slots_t, ((0, depth - deg), (0, 0)), constant_values=-1)
    slots = jnp.where(step < counts[None, :], slots, -1)
    return slots.reshape(depth, groups, GROUP).transpose(1, 0, 2).reshape(groups, SPAN)


def incidence(slots, widths, after, made=None, batch=8):
    groups = slots.shape[0]
    nodes = groups * GROUP
    total = sum(widths)
    block = batch * GROUP
    steps = groups // batch // 2
    first = 0 if made is None else steps
    made = made or ()
    waits = len(made) + len(after)
    *weights, token = pl.pallas_call(
        functools.partial(incidence_kernel, waits),
        grid=(steps,),
        in_specs=[pl.BlockSpec((batch, SPAN), lambda i: (i + first, 0))]
        + [pl.BlockSpec(memory_space=pl.ANY)] * waits,
        out_specs=[pl.BlockSpec((block, w), lambda i: (i + first, 0)) for w in widths]
        + [pl.BlockSpec((8, 128), lambda i: (0, 0))],
        out_shape=[jax.ShapeDtypeStruct((nodes, w), jnp.bfloat16) for w in widths]
        + [jax.ShapeDtypeStruct((8, 128), jnp.int32)],
        input_output_aliases={1 + i: i for i in range(len(made))},
        cost_estimate=pl.CostEstimate(
            flops=nodes, bytes_accessed=nodes, transcendentals=0
        ),
        compiler_params=pltpu.CompilerParams(vmem_limit_bytes=56 << 20),
        name="incidence",
    )(slots, *made, *after)
    return weights, token[0, 0]


def layer_kernel(core_ref, own, own_far, mean, mean_far, w_self, w_self_far, w_neigh, w_neigh_far,
                 cotangent_ref, out_ref, mine_ref, other_ref, total_ref):
    step = pl.program_id(0)

    def product(rows, weight):
        return jnp.dot(rows[...], weight[...], preferred_element_type=jnp.float32)

    pre = (product(own, w_self) + product(own_far, w_self_far)) + (
        product(mean, w_neigh) + product(mean_far, w_neigh_far)
    )
    scale = math.sqrt(2 / math.pi)
    square = pre * pre
    tanh = jnp.tanh(scale * (pre + 0.044715 * (square * pre)))
    half_up = 0.5 * (1.0 + tanh)
    out_ref[...] = (pre * half_up).astype(jnp.bfloat16)
    slope = half_up + 0.5 * pre * (1.0 - tanh * tanh) * (scale * (1.0 + 3 * 0.044715 * square))
    grad = (cotangent_ref[...].astype(jnp.float32) * slope).astype(jnp.bfloat16)
    part = jnp.concatenate(
        [
            lax.dot_general(
                grad, rows[...], (((0,), (0,)), ((), ())), preferred_element_type=jnp.float32
            )
            for rows in (own, mean, own_far, mean_far)
        ],
        1,
    )

    @pl.when(step == 0)
    def _():
        total_ref[...] = part

    @pl.when(step > 0)
    def _():
        total_ref[...] += part

    @pl.when(step == pl.num_programs(0) - 1)
    def _():
        total = total_ref[...].T.astype(jnp.bfloat16)
        mine_ref[...] = total[:mine_ref.shape[0]]
        other_ref[...] = total[mine_ref.shape[0]:]


def layer(core, own, own_far, mean, mean_far, w_self, w_neigh, weights_far, cotangent, block=256):
    nodes, half = own.shape
    rows = pl.BlockSpec((block, half), lambda i, c: (i, 0))

    def weight(place):
        return pl.BlockSpec((half, half), lambda i, c: (place, c[0]), pipeline_mode=pl.Buffered(1))

    whole = pl.BlockSpec((2 * half, half), lambda i, c: (0, 0))
    return pl.pallas_call(
        layer_kernel,
        grid_spec=pltpu.PrefetchScalarGridSpec(
            num_scalar_prefetch=1,
            grid=(nodes // block,),
            in_specs=[rows] * 4 + [weight(0), weight(0), weight(0), weight(1), rows],
            out_specs=[rows, whole, whole],
            scratch_shapes=[pltpu.VMEM((half, 4 * half), jnp.float32)],
        ),
        out_shape=[
            jax.ShapeDtypeStruct((nodes, half), jnp.bfloat16),
            jax.ShapeDtypeStruct((2 * half, half), jnp.bfloat16),
            jax.ShapeDtypeStruct((2 * half, half), jnp.bfloat16),
        ],
        cost_estimate=pl.CostEstimate(
            flops=16 * nodes * half * half, bytes_accessed=12 * nodes * half, transcendentals=nodes * half
        ),
        compiler_params=pltpu.CompilerParams(vmem_limit_bytes=24 << 20),
        name="layer",
    )(core, own, own_far, mean, mean_far, w_self, weights_far, w_neigh, weights_far, cotangent)


def swap(value):
    return lax.ppermute(value, "col", SWAP)


def shift(value, axis, offset):
    stride, size = LINES[axis]
    pairs = []
    for source in range(128):
        here = source // stride % size
        pairs.append((source, source + ((here + offset) % size - here) * stride))
    return lax.ppermute(value, "dom", pairs)


def exchange(blocks, axes):
    fixed = [(stride, size) for axis, (stride, size) in LINES.items() if axis not in axes]
    moving = [LINES[axis] for axis in axes]

    def spots(lines):
        found = [0]
        for stride, size in lines:
            found = [spot + step * stride for spot in found for step in range(size)]
        return found

    groups = [[base + spot for spot in spots(moving)] for base in spots(fixed)]
    return lax.all_to_all(
        blocks, "dom", split_axis=0, concat_axis=0, tiled=True, axis_index_groups=groups
    )


def share(block, axes):
    count = math.prod(LINES[axis][1] for axis in axes)
    return exchange(jnp.broadcast_to(block[None], (count,) + block.shape), axes)


def spread_y(line, token):
    rows = [line] + [shift(line, "y", -ahead) for ahead in (1, 2, 3)]
    return jnp.concatenate(rows, 0) + token.astype(line.dtype)


def opposite(after, before, token):
    middle = after.shape[0] // 2
    zero = token.astype(after.dtype)
    return jnp.concatenate(
        [shift(after[:middle] + zero, "x", -1), shift(before[middle:] + zero, "x", 1)], 0
    )


def table_order(slots, nodes, hubs):
    here = lax.axis_index("dom")
    hub = slots - nodes
    owner = hub >> 5
    ahead_x = ((owner >> 5) - (here >> 5)) & 3
    ahead_x = ahead_x ^ (ahead_x >> 1)
    ahead_y = ((owner >> 3) - (here >> 3)) & 3
    moved = nodes + ((ahead_x * 4 + ahead_y) << 8) + (hub & 255)
    return jnp.where((hub >= 0) & (hub < hubs), moved, slots)


def dot(left, right):
    return jnp.dot(left, right, preferred_element_type=jnp.float32)


def shards(features, cotangent, w_self, w_neigh, hub_rows, send_rows, neighbours, counts):
    parts = lax.axis_size("dom")
    nodes, half = features.shape
    core = lax.axis_index("col")
    features_far, weights_far = swap(features), swap(jnp.concatenate([w_self, w_neigh], 0))
    lanes = jnp.arange(nodes, dtype=jnp.int32)[None, :]

    def pick(rows):
        onehot = (rows[:, None] == lanes).astype(jnp.bfloat16)
        return dot(onehot, features).astype(jnp.bfloat16)

    hubs = parts * hub_rows.shape[0]
    slots = pack_slots(table_order(neighbours.T, nodes, hubs), counts)
    widths = (nodes,) + (hubs // 4,) * 4 + (parts * send_rows.shape[2],)
    outgoing = pick(send_rows.reshape(-1))
    incoming = lax.all_to_all(
        outgoing.reshape(parts, -1, half), "dom", split_axis=0, concat_axis=0, tiled=True
    ).reshape(-1, half)
    line = share(pick(hub_rows), "z").reshape(-1, half)
    made, token = incidence(slots, widths, (line,))
    plane = spread_y(line, token)
    after, before = shift(plane, "x", -1), shift(plane, "x", 1)
    weights, token = incidence(slots, widths, (plane, features_far, weights_far), made)
    far = opposite(after, before, token)
    fence = lax.optimization_barrier
    total = fence(dot(weights[2], after))
    for weight, rows in zip((weights[3], weights[1], weights[0]), (before, plane, features)):
        total = fence(total + dot(weight, rows))
    total = fence(total + dot(weights[4], far))
    total = total + dot(weights[5], incoming)
    neigh_mean = (total / counts[:, None].astype(jnp.float32)).astype(jnp.bfloat16)
    mean_far = swap(neigh_mean)
    layer_out, mine, other = layer(
        core.astype(jnp.int32).reshape(1), features, features_far, neigh_mean, mean_far,
        w_self, w_neigh, weights_far, cotangent,
    )
    partial = jnp.concatenate([mine, swap(other)], 0).reshape(16, -1, half)

    def added(pieces):
        return pieces.astype(jnp.float32).sum(0)

    piece = added(exchange(partial, "xy")).astype(jnp.bfloat16)
    factor = 1.0 / math.sqrt(nodes * parts)
    piece = (added(share(piece, "z")) * factor).astype(jnp.bfloat16)
    sums = share(piece, "xy").reshape(2, 2, half, half).astype(jnp.float32)
    low = jnp.where(core == 0, sums[0], sums[1])
    high = jnp.where(core == 0, sums[1], sums[0])
    return (
        layer_out,
        jnp.concatenate([low[0], high[0]], 1),
        jnp.concatenate([low[1], high[1]], 1),
    )


def solution(mesh):
    placed = (
        P("dom", "col"),
        P("dom", "col"),
        P("col", None),
        P("col", None),
        P("dom"),
        P("dom", None, None),
        P("dom", None),
        P("dom"),
    )
    return jax.shard_map(
        shards,
        mesh=mesh,
        in_specs=placed,
        out_specs=(P("dom", "col"), P("col", None), P("col", None)),
        check_vma=False,
    )
```
